32 devices in a mesh: groups: 2 (over y), ctx: 4 (over z), section: 2 (over x), head: 2 (over core).
Axes of the slice: x: 2, y: 2, z: 4, core: 2. Of those that a mesh axis runs over, the one named last changes fastest.
Arguments:
- tokens: bfloat16 [4, 512, 2048], P('groups', 'ctx', 'head'), parts along dimension 0, may hold values from -20 to 20
- norm_gain: bfloat16 [2, 2048], P('section'), may hold values from 0.5 to 1.5
- w_query: bfloat16 [2, 2048, 256], P('section', None, 'head'), may hold values from -0.125 to 0.125
- w_key: bfloat16 [2, 2048, 256], P('section', None, 'head'), may hold values from -0.125 to 0.125
- w_value: bfloat16 [2, 2048, 2048], P('section', None, 'head'), may hold values from -0.125 to 0.125
- conv_query: bfloat16 [2, 4, 256], P('section', None, 'head'), may hold values from -3 to 3
- conv_key: bfloat16 [2, 4, 256], P('section', None, 'head'), may hold values from -3 to 3
- conv_value: bfloat16 [2, 4, 2048], P('section', None, 'head'), may hold values from -3 to 3
- value_gain: bfloat16 [2, 2048], P('section', 'head'), may hold values from 0.5 to 1.5
- w_out: bfloat16 [2, 2048, 2048], P('section', 'head'), may hold values from -0.125 to 0.125
- doc_start: int32 [4], P('groups'), parts along dimension 0, may hold values from 1 to 511
- pad_length: int32 [4], P('groups'), parts along dimension 0, may hold values from 0 to 255
Outputs:
- layer_outputs: bfloat16 [2, 4, 512, 2048], P('section', 'groups', 'ctx', 'head'), parts along dimension 1
The draws below stay inside these ranges and needn't reach their ends.
There are 2 independent parts, one for each index of `groups`. The reference program is written for one: setup_inputs(seed, part) draws one part's arguments, and reference() takes and returns one part's arrays. A program takes and returns all parts, laid end to end along the dimension named above; an argument that names none is the same for every part. Nothing has to cross between parts.
All inputs are finite; a program needn't handle non-finite values.
Results may differ from the reference program's by a relative error of at most 0.0061.
Values may be sent and summed in bfloat16 or wider, within the bound.
A program may use at most 128 MiB of HBM per device.

```python
import math
import jax
import jax.numpy as jnp
import numpy as np
from jax import lax

D = 2048
HEADS = 16
FD = 16
HD = 128
FEAT = 153
KCONV = 4
SPAN = 128
MICRO = 2
WINDOW = 512
LAYERS = 2


def draw_tokens(key, part):
    key_rows, key_cols, key_main = jax.random.split(key, 3)
    row_scale = jnp.exp(jax.random.uniform(key_rows, (MICRO, WINDOW, 1), jnp.float32, math.log(0.7), math.log(1.4)))
    col_scale = jnp.exp(jax.random.uniform(key_cols, (1, 1, D), jnp.float32, math.log(0.35), math.log(3.5)))
    values = jnp.clip(jax.random.normal(key_main, (MICRO, WINDOW, D), jnp.float32), -4.0, 4.0)
    return (values * row_scale * col_scale).astype(jnp.bfloat16)


def steps_of(own_key, shape, cuts, smallest, top_value):
    def one(position, parts):
        steps = jax.random.uniform(jax.random.fold_in(jax.random.fold_in(own_key, 6), position), (parts,), jnp.float32, smallest / len(cuts), top_value / len(cuts))
        return jnp.repeat(jnp.exp(steps), shape[position] // parts).reshape((-1,) + (1,) * (len(shape) - position - 1))

    factor_of = one(*cuts[0])
    for cut in cuts[1:]:
        factor_of = factor_of * one(*cut)
    return factor_of


def bell_draw(rng, dims, deviation, most, cuts=(), kind=jnp.bfloat16):
    entries = jax.random.normal(rng, dims, jnp.float32) * deviation
    if len(cuts) > 0:
        entries = steps_of(rng, dims, cuts, -0.22, 0.18) * entries
    return jnp.clip(entries, min=-most, max=most).astype(kind)


def setup_inputs(seed: int = 0, part: int = 0) -> dict:
    key_list = jax.random.split(jax.random.key(seed), 13)
    part_splits = jax.random.split(jax.random.fold_in(key_list[12], part), 13)
    tokens = draw_tokens(jax.random.fold_in(jax.random.fold_in(key_list[12], part), 71), part)
    norm_gain = jnp.clip(1.0 + 0.1 * jax.random.normal(key_list[1], (LAYERS, D), jnp.float32), 0.5, 1.5).astype(jnp.bfloat16)
    w_query = bell_draw(key_list[2], (LAYERS, D, HEADS * FD), D ** -0.5, 0.125, ((0, 2), (2, 2)))
    w_key = bell_draw(key_list[3], (LAYERS, D, HEADS * FD), D ** -0.5, 0.125, ((0, 2), (2, 2)))
    w_value = bell_draw(key_list[4], (LAYERS, D, HEADS * HD), D ** -0.5, 0.125, ((0, 2), (2, 2)))
    conv_query = bell_draw(key_list[5], (LAYERS, KCONV, HEADS * FD), KCONV ** -0.5, 3.0, ((0, 2), (2, 2)))
    conv_key = bell_draw(key_list[6], (LAYERS, KCONV, HEADS * FD), KCONV ** -0.5, 3.0, ((0, 2), (2, 2)))
    conv_value = bell_draw(key_list[7], (LAYERS, KCONV, HEADS * HD), KCONV ** -0.5, 3.0, ((0, 2), (2, 2)))
    value_gain = jnp.clip(1.0 + 0.1 * jax.random.normal(key_list[8], (LAYERS, HEADS * HD), jnp.float32), 0.5, 1.5).astype(jnp.bfloat16)
    w_out = bell_draw(key_list[9], (LAYERS, HEADS * HD, D), (HEADS * HD) ** -0.5, 0.125, ((0, 2), (1, 2)))
    doc_start = jax.random.randint(part_splits[10], (MICRO,), 1, WINDOW).astype(jnp.int32)
    pad_length = jax.random.randint(part_splits[11], (MICRO,), 0, 2 * SPAN).astype(jnp.int32)
    return dict(tokens=tokens, norm_gain=norm_gain, w_query=w_query, w_key=w_key, w_value=w_value, conv_query=conv_query, conv_key=conv_key, conv_value=conv_value, value_gain=value_gain, w_out=w_out, doc_start=doc_start, pad_length=pad_length)


norm_eps = 1e-06

def pair_tables(feat_width):
    left_list = []
    right_list = []
    weight_list = []
    for left_pos in range(feat_width):
        for right_pos in range(left_pos, feat_width):
            left_list.append(left_pos)
            right_list.append(right_pos)
            if left_pos == right_pos:
                weight_list.append(1.0 / math.sqrt(2.0 * feat_width))
            else:
                weight_list.append(1.0 / math.sqrt(feat_width))
    return (np.array(left_list, np.int32), np.array(right_list, np.int32), weight_list)

def taylor_features(vectors):
    feat_width = vectors.shape[-1]
    left_index, right_index, weight_list = pair_tables(feat_width)
    pair_weight = jnp.asarray(weight_list, dtype=jnp.float32)
    constant = jnp.ones(vectors.shape[:-1] + (1,), jnp.float32)
    linear = vectors * (1.0 / feat_width ** 0.25)
    quadratic = vectors[..., left_index] * vectors[..., right_index] * pair_weight
    return jnp.concatenate([constant, linear, quadratic], axis=-1)

def normed_rows(hidden, gain):
    row_values = hidden.astype(jnp.float32)
    mean_square = lax.optimization_barrier(jnp.mean(row_values * row_values, axis=-1, keepdims=True))
    return (row_values * lax.rsqrt(mean_square + norm_eps) * gain.astype(jnp.float32)).astype(jnp.bfloat16)

def short_conv(extended, tap_weights, positions, boundary):
    tap_count = tap_weights.shape[0]
    row_count = extended.shape[0] - tap_count + 1
    summed = jnp.zeros((row_count, extended.shape[1]), jnp.float32)
    after_start = positions >= boundary
    for offset in range(tap_count):
        source = extended[tap_count - 1 - offset:tap_count - 1 - offset + row_count].astype(jnp.float32)
        earlier_side = positions - offset >= boundary
        keep_rows = (earlier_side == after_start).astype(jnp.float32)
        summed = summed + tap_weights[offset].astype(jnp.float32) * source * keep_rows[:, None]
    return summed

def mix_rows(queries, key_vals, values, positions, boundary, carried, value_gain):
    row_count = queries.shape[0]
    head_count = values.shape[1] // HD
    query_heads = queries.reshape(row_count, head_count, -1)
    key_heads = key_vals.reshape(row_count, head_count, -1)
    value_heads = values.reshape(row_count, head_count, HD)
    feat_width = query_heads.shape[-1]
    scores = jnp.einsum('ihd,jhd->hij', query_heads, key_heads, precision=lax.Precision.HIGHEST) / math.sqrt(feat_width)
    after_start = positions >= boundary
    allowed = (positions[None, :] <= positions[:, None]) & (after_start[None, :] == after_start[:, None])
    weights = jnp.where(allowed[None], 1.0 + scores + 0.5 * scores * scores, 0.0).astype(jnp.bfloat16)
    local_part = jnp.einsum('hij,jhd->ihd', weights.astype(jnp.float32), value_heads.astype(jnp.float32))
    block_start = positions[0]
    use_carried = (positions < boundary) | (boundary < block_start)
    query_feats = taylor_features(query_heads)
    far_part = jnp.einsum('ihf,hfd->ihd', query_feats, carried, precision=lax.Precision.HIGHEST)
    far_part = far_part * use_carried.astype(jnp.float32)[:, None, None]
    numerator = local_part + far_part
    mean_square = lax.optimization_barrier(jnp.mean(numerator * numerator, axis=-1, keepdims=True))
    scaled = numerator * lax.rsqrt(mean_square + norm_eps)
    return (scaled.reshape(row_count, -1) * value_gain.astype(jnp.float32)).astype(jnp.bfloat16)

def local_state(key_vals, values, positions, boundary):
    row_count = key_vals.shape[0]
    head_count = values.shape[1] // HD
    key_heads = key_vals.reshape(row_count, head_count, -1)
    value_heads = values.reshape(row_count, head_count, HD)
    block_start = positions[0]
    reset_here = (boundary >= block_start) & (boundary < block_start + row_count)
    keep_keys = (positions >= boundary) | jnp.logical_not(reset_here)
    key_feats = (taylor_features(key_heads) * keep_keys.astype(jnp.float32)[:, None, None]).astype(jnp.bfloat16)
    block_state = jnp.einsum('jhf,jhd->hfd', key_feats.astype(jnp.float32), value_heads.astype(jnp.float32))
    return (block_state, reset_here)

def apply_layer(hidden, gain_norm, weight_query, weight_key, weight_value, taps_query, taps_key, taps_value, gain_value, weight_out, boundary, pad_count):
    window_rows = hidden.shape[0]
    positions = jnp.arange(window_rows, dtype=jnp.int32)
    normed = normed_rows(hidden, gain_norm)
    rim_rows = taps_query.shape[0] - 1

    def project_conv(weight_matrix, tap_weights):
        projected_rows = jnp.dot(normed, weight_matrix, preferred_element_type=jnp.float32).astype(jnp.bfloat16)
        extended = jnp.concatenate([jnp.zeros((rim_rows, projected_rows.shape[1]), jnp.bfloat16), projected_rows], axis=0)
        return short_conv(extended, tap_weights, positions, boundary)
    queries = project_conv(weight_query, taps_query)
    key_vals = project_conv(weight_key, taps_key)
    values = project_conv(weight_value, taps_value).astype(jnp.bfloat16)
    block_count = window_rows // SPAN

    def step_block(carried, block_pos):
        first_row = (block_pos * SPAN).astype(jnp.int32)
        block_queries = lax.dynamic_slice_in_dim(queries, first_row, SPAN, 0)
        block_keys = lax.dynamic_slice_in_dim(key_vals, first_row, SPAN, 0)
        block_values = lax.dynamic_slice_in_dim(values, first_row, SPAN, 0)
        block_positions = first_row + jnp.arange(SPAN, dtype=jnp.int32)
        mixed_rows = mix_rows(block_queries, block_keys, block_values, block_positions, boundary, carried, gain_value)
        block_state, reset_here = local_state(block_keys, block_values, block_positions, boundary)
        next_state = block_state + jnp.where(reset_here, 0.0, 1.0) * carried
        return (next_state, mixed_rows)
    start_state = jnp.zeros((HEADS, FEAT, HD), jnp.float32)
    final_state, mixed_blocks = lax.scan(step_block, start_state, jnp.arange(block_count, dtype=jnp.int32))
    mixed_all = mixed_blocks.reshape(window_rows, -1)
    update = jnp.dot(mixed_all, weight_out, preferred_element_type=jnp.float32)
    valid_rows = (positions < window_rows - pad_count).astype(jnp.float32)[:, None]
    return (hidden.astype(jnp.float32) + update * valid_rows).astype(jnp.bfloat16)

def reference(tokens, norm_gain, w_query, w_key, w_value, conv_query, conv_key, conv_value, value_gain, w_out, doc_start, pad_length):
    results = []
    for layer_pos in range(LAYERS):
        layer_rows_out = []
        for micro_pos in range(MICRO):
            if layer_pos == 0:
                hidden = tokens[micro_pos]
            else:
                hidden = results[layer_pos - 1][micro_pos]
            layer_rows_out.append(apply_layer(hidden, norm_gain[layer_pos], w_query[layer_pos], w_key[layer_pos], w_value[layer_pos], conv_query[layer_pos], conv_key[layer_pos], conv_value[layer_pos], value_gain[layer_pos], w_out[layer_pos], doc_start[micro_pos], pad_length[micro_pos]))
        results.append(jnp.stack(layer_rows_out))
    return jnp.stack(results)
```

```python
import math

import jax
import jax.numpy as jnp
from jax import lax
from jax.experimental import pallas as pl
from jax.experimental.pallas import tpu as pltpu
from jax.sharding import PartitionSpec as P

HD = 128
FD = 16
FROWS = 160
CHUNK = 256
EPS = 1e-06
MESH = pl.DeviceIdType.MESH
F32 = jnp.float32
BF16 = jnp.bfloat16


def features(doubled, h, lead):
    y = doubled[h, pl.ds(0, FD), :]
    rows = [y, y * y * math.sqrt(0.5)]
    for d in range(1, FD // 2):
        rows.append(y * doubled[h, pl.ds(d, FD), :])
    half = FD // 2
    rows.append(y[:half] * y[half:])
    top = lax.broadcasted_iota(jnp.int32, (half, y.shape[1]), 0) == 0
    rows.append(jnp.where(top, lead, 0.0))
    return jnp.concatenate(rows, axis=0).astype(BF16)


def make_kernel(sizes):
    ctx_n, sec_n, windows, span, width, taps = sizes
    half = width // 2
    heads = half // HD
    vchunks = half // CHUNK
    pair = heads // vchunks
    wide = CHUNK // HD

    def kernel(
        start_in, pad_in, tok_in, gain_in, wq_ref, wk_ref, wv_ref, cq_in, ck_in, cv_in, vg_in, wo_ref,
        out_hbm,
        start_ref, pad_ref, gain_ref, cq_ref, ck_ref, cv_ref, vg_ref, small_sem,
        w_all, wo_v, x_ref, n_ref, pr_ref, ho_ref, hi_ref, q3_ref, k3_ref, qt_ref, kt_ref, v_ref,
        bs_ref, got_ref, fwd_ref, qf_ref, num_ref, mix_ref, mask_ref, part_ref, other_ref, o_ref,
        w_sem, tok_sem, out_sem, x_send, x_recv, sec_send, sec_recv, halo_send, halo_recv, st_send, st_recv,
        p_send, p_recv,
    ):
        ctx = lax.axis_index("ctx")
        sec = lax.axis_index("section")
        core = lax.axis_index("head")
        mate = 1 - core

        def cols(j):
            return pl.ds(j * CHUNK, CHUNK)

        def rows(m):
            return pl.ds(pl.multiple_of(m * span, span), span)

        def head_lanes(h):
            return pl.ds(pl.multiple_of(h * HD, HD), HD)

        def tok_load(m, j):
            return pltpu.make_async_copy(
                tok_in.at[rows(m), cols(j)], x_ref.at[m, core * vchunks + j], tok_sem.at[m, j]
            )

        @pl.when(sec == 0)
        def _():
            for m in range(windows):
                for j in range(vchunks):
                    tok_load(m, j).start()

        small = [
            pltpu.make_async_copy(source, target, small_sem.at[i])
            for i, (source, target) in enumerate(
                (
                    (gain_in, gain_ref),
                    (start_in, start_ref),
                    (pad_in, pad_ref),
                    (cq_in, cq_ref),
                    (ck_in, ck_ref),
                    (cv_in, cv_ref),
                    (vg_in, vg_ref),
                )
            )
        ]
        for load in small:
            load.start()

        loads = [
            pltpu.make_async_copy(wq_ref.at[0], w_all.at[0, :, pl.ds(0, HD)], w_sem.at[0]),
            pltpu.make_async_copy(wk_ref.at[0], w_all.at[0, :, pl.ds(HD, HD)], w_sem.at[1]),
        ]
        for j in range(vchunks):
            loads.append(pltpu.make_async_copy(wv_ref.at[0, :, cols(j)], w_all.at[1 + j], w_sem.at[2 + j]))
        for j in range(2 * vchunks):
            loads.append(pltpu.make_async_copy(wo_ref.at[0, :, cols(j)], wo_v.at[j], w_sem.at[2 + vchunks + j]))
        for load in loads:
            load.start()

        barrier = pltpu.get_barrier_semaphore()
        pl.semaphore_signal(barrier, inc=1, device_id={"head": mate}, device_id_type=MESH)

        @pl.when(ctx > 0)
        def _():
            pl.semaphore_signal(barrier, inc=1, device_id={"ctx": ctx - 1}, device_id_type=MESH)

        @pl.when(ctx < ctx_n - 1)
        def _():
            pl.semaphore_signal(barrier, inc=1, device_id={"ctx": ctx + 1}, device_id_type=MESH)

        @pl.when(sec > 0)
        def _():
            pl.semaphore_signal(barrier, inc=1, device_id={"section": sec - 1}, device_id_type=MESH)

        @pl.when(sec < sec_n - 1)
        def _():
            pl.semaphore_signal(barrier, inc=1, device_id={"section": sec + 1}, device_id_type=MESH)

        first = ctx * span
        lead_pos = lax.broadcasted_iota(jnp.int32, (1, span), 1) + first
        col_pos = lax.broadcasted_iota(jnp.int32, (span, HD), 0) + first
        lane = lax.broadcasted_iota(jnp.int32, (1, HD), 1)
        low_half = lane < HD // 2
        lane_head = (lax.broadcasted_iota(jnp.int32, (1, 2 * HD), 1) % (HD // 2)) // FD

        @pl.when(ctx == 0)
        def _():
            pr_ref[:, pl.ds(0, 8), :] = jnp.zeros((half // HD + wide, 8, HD), F32)

            def clear(i, carry):
                got_ref[i // heads, i % heads] = jnp.zeros((FROWS, HD), BF16)
                return carry

            lax.fori_loop(0, windows * heads, clear, 0)

        peers = (
            1
            + jnp.where(ctx > 0, 1, 0)
            + jnp.where(ctx < ctx_n - 1, 1, 0)
            + jnp.where(sec > 0, 1, 0)
            + jnp.where(sec < sec_n - 1, 1, 0)
        )
        pl.semaphore_wait(barrier, peers)

        def section_copy(m, j):
            return pltpu.make_async_remote_copy(
                src_ref=o_ref.at[m, j],
                dst_ref=x_ref.at[m, core * vchunks + j],
                send_sem=sec_send.at[m, j],
                recv_sem=sec_recv.at[m, j],
                device_id={"section": sec + 1},
                device_id_type=MESH,
            )

        def mate_copy(m, j):
            return pltpu.make_async_remote_copy(
                src_ref=x_ref.at[m, core * vchunks + j],
                dst_ref=x_ref.at[m, core * vchunks + j],
                send_sem=x_send.at[m, j],
                recv_sem=x_recv.at[m, j],
                device_id={"head": mate},
                device_id_type=MESH,
            )

        def halo_copy(m, j):
            return pltpu.make_async_remote_copy(
                src_ref=ho_ref.at[m, j],
                dst_ref=hi_ref.at[m, j],
                send_sem=halo_send.at[m, j],
                recv_sem=halo_recv.at[m, j],
                device_id={"ctx": ctx + 1},
                device_id_type=MESH,
            )

        def state_copy(m, h):
            return pltpu.make_async_remote_copy(
                src_ref=fwd_ref.at[m, h],
                dst_ref=got_ref.at[m, h],
                send_sem=st_send.at[m, h],
                recv_sem=st_recv.at[m, h],
                device_id={"ctx": ctx + 1},
                device_id_type=MESH,
            )

        def part_copy(m, j):
            return pltpu.make_async_remote_copy(
                src_ref=part_ref.at[m, j],
                dst_ref=other_ref.at[m, j],
                send_sem=p_send.at[m, j],
                recv_sem=p_recv.at[m, j],
                device_id={"head": mate},
                device_id_type=MESH,
            )

        def out_copy(m, j):
            return pltpu.make_async_copy(o_ref.at[m, j], out_hbm.at[rows(m), cols(j)], out_sem.at[m, j])

        def exchange(m):
            for j in range(vchunks):

                @pl.when(sec == 0)
                def _():
                    tok_load(m, j).wait()

                @pl.when(sec > 0)
                def _():
                    section_copy(m, j).wait_recv()

                mate_copy(m, j).start()

        exchange(0)

        for load in small:
            load.wait()

        def normalise(m):
            parts = []
            for k in range(2 * vchunks):
                value = x_ref[m, k].astype(F32)
                square = value * value
                for c in range(wide):
                    parts.append(square[:, c * HD : (c + 1) * HD])
            total = parts[0]
            for part in parts[1:]:
                total = total + part
            scale = lax.rsqrt(jnp.sum(total, axis=1, keepdims=True) * (1.0 / width) + EPS)
            for k in range(2 * vchunks):
                gain = gain_ref[:, cols(k)].astype(F32)
                n_ref[k] = (x_ref[m, k].astype(F32) * scale * gain).astype(BF16)

        def project(m, j):
            normed = jnp.concatenate([n_ref[k] for k in range(2 * vchunks)], axis=1)
            got = jnp.dot(normed, w_all[j], preferred_element_type=F32).astype(BF16).astype(F32)
            for c in range(wide):
                pr_ref[wide * j + c, pl.ds(8, span), :] = got[:, c * HD : (c + 1) * HD]
                ho_ref[m, j, pl.ds(4 * c, 4), :] = got[span - 4 :, c * HD : (c + 1) * HD]

        def halo_send_off(m, j):
            @pl.when(ctx < ctx_n - 1)
            def _():
                halo_copy(m, j).start()

        def halo_wait(m, j):
            @pl.when(ctx > 0)
            def _():
                halo_copy(m, j).wait_recv()
                for c in range(wide):
                    pr_ref[wide * j + c, pl.ds(4, 4), :] = hi_ref[m, j, pl.ds(4 * c, 4), :]

        def conv(c, taps_ref, tap_at, since):
            total = taps_ref[0, pl.ds(0, 1), tap_at].astype(F32) * pr_ref[c, pl.ds(8, span), :]
            for j in range(1, taps):
                term = taps_ref[0, pl.ds(j, 1), tap_at].astype(F32) * pr_ref[c, pl.ds(8 - j, span), :]
                total = total + jnp.where(since >= j, term, 0.0)
            return total

        def window(m, carry):
            start = start_ref[m]
            inside = jnp.logical_and(start >= first, start < first + span)
            since = col_pos - start
            since = jnp.where(since < 0, taps, since)
            kept = jnp.where(jnp.logical_or(lead_pos >= start, jnp.logical_not(inside)), 1.0, 0.0)
            used = jnp.where(jnp.logical_or(lead_pos < start, start < first), 1.0, 0.0)

            for j in range(vchunks):
                mate_copy(m, j).wait_recv()
            normalise(m)

            def conv_query_key():
                for which, taps_ref, wide_ref, turned_ref, lead in (
                    (1, ck_ref, k3_ref, kt_ref, kept),
                    (0, cq_ref, q3_ref, qt_ref, used),
                ):
                    part = conv(which, taps_ref, pl.ds(0, HD), since)
                    turned = jnp.transpose(part) * (0.5 * lead)
                    for h in range(heads):
                        own = turned[h * FD : (h + 1) * FD]
                        turned_ref[h, pl.ds(0, FD), :] = own
                        turned_ref[h, pl.ds(FD, FD), :] = own
                    if which == 0:
                        part = part * (1.0 / math.sqrt(FD))
                    rolled = pltpu.roll(part, HD // 2, 1)
                    for g in range(2):
                        both = jnp.where(low_half, part, rolled) if g == 0 else jnp.where(low_half, rolled, part)
                        high = both.astype(BF16).astype(F32)
                        low = both - high
                        if which == 0:
                            wide_ref[g, :, pl.ds(0, HD)] = high.astype(BF16)
                            wide_ref[g, :, pl.ds(HD, HD)] = low.astype(BF16)
                        else:
                            wide_ref[g, :, pl.ds(0, HD)] = jnp.where(low_half, high, low).astype(BF16)
                            wide_ref[g, :, pl.ds(HD, HD)] = jnp.where(low_half, high, 0.0).astype(BF16)

            def values(j):
                for c in range(wide):
                    h = wide * j + c
                    v_ref[h] = conv(wide + h, cv_ref, pl.ds(h * HD, HD), since).astype(BF16)
                    made = jnp.dot(features(kt_ref, h, kept), v_ref[h], preferred_element_type=F32)
                    fwd_ref[m, h] = made.astype(BF16)
                    bs_ref[h] = made

            def send_states(j):
                if ctx_n > 1:

                    @pl.when(ctx == 0)
                    def _():
                        for c in range(pair):
                            state_copy(m, pair * j + c).start()

            def weights_ready(j):
                @pl.when(m == 0)
                def _():
                    if j == 0:
                        loads[0].wait()
                    loads[1 + j].wait()

            weights_ready(0)
            project(m, 0)
            halo_send_off(m, 0)
            weights_ready(1)
            halo_wait(m, 0)
            project(m, 1)
            conv_query_key()
            halo_send_off(m, 1)
            for j in range(vchunks):
                if j + 2 <= vchunks:
                    weights_ready(j + 2)
                halo_wait(m, j + 1)
                if j + 2 <= vchunks:
                    project(m, j + 2)
                values(j)
                if j + 2 <= vchunks:
                    halo_send_off(m, j + 2)
                send_states(j)

            edge = start - first
            row_pos = lax.broadcasted_iota(jnp.int32, (span, span), 0)
            other_pos = lax.broadcasted_iota(jnp.int32, (span, span), 1)
            allowed = jnp.logical_and(other_pos <= row_pos, (other_pos >= edge) == (row_pos >= edge))
            mask_ref[...] = jnp.where(allowed, 1.0, 0.0).astype(BF16)

            def local_part(g, carry):
                for c in range(heads // 2):
                    h = g * (heads // 2) + c
                    mine = jnp.where(lane_head == c, q3_ref[g], jnp.zeros((), BF16))
                    s = lax.dot_general(mine, k3_ref[g], (((1,), (1,)), ((), ())), preferred_element_type=F32)
                    weight = ((0.5 * s + 1.0) * s + 1.0).astype(BF16) * mask_ref[...]
                    num_ref[h] = jnp.dot(weight, v_ref[h], preferred_element_type=F32)
                    qf_ref[h] = jnp.transpose(features(qt_ref, h, used))
                return carry

            lax.fori_loop(0, 2, local_part, 0)

            def chain(h, carry):
                @pl.when(ctx > 0)
                def _():
                    state_copy(m, h).wait_recv()

                @pl.when(jnp.logical_and(ctx > 0, ctx < ctx_n - 1))
                def _():
                    old = got_ref[m, h].astype(F32)
                    fwd_ref[m, h] = (bs_ref[h] + jnp.where(inside, 0.0, old)).astype(BF16)
                    state_copy(m, h).start()

                num = num_ref[h] + jnp.dot(qf_ref[h], got_ref[m, h], preferred_element_type=F32)
                square = jnp.mean(num * num, axis=1, keepdims=True)
                mix_ref[h] = (num * lax.rsqrt(square + EPS) * vg_ref[:, head_lanes(h)].astype(F32)).astype(BF16)
                return carry

            lax.fori_loop(0, heads, chain, 0)

            @pl.when(m < windows - 1)
            def _():
                exchange(m + 1)

            @pl.when(m == 0)
            def _():
                for j in range(2 * vchunks):
                    loads[2 + vchunks + j].wait()

            mixed = jnp.concatenate([mix_ref[h] for h in range(heads)], axis=1)
            for j in range(vchunks):
                part_ref[m, j] = jnp.dot(mixed, wo_v[mate * vchunks + j], preferred_element_type=F32)
                part_copy(m, j).start()
            valid = first + lax.broadcasted_iota(jnp.int32, (span, CHUNK), 0) < span * ctx_n - pad_ref[m]
            for j in range(vchunks):
                mixed = jnp.concatenate([mix_ref[h] for h in range(heads)], axis=1)
                mine = jnp.dot(mixed, wo_v[core * vchunks + j], preferred_element_type=F32)
                part_copy(m, j).wait_recv()
                update = jnp.where(valid, mine + other_ref[m, j], 0.0)
                o_ref[m, j] = (x_ref[m, core * vchunks + j].astype(F32) + update).astype(BF16)

                @pl.when(sec < sec_n - 1)
                def _():
                    section_copy(m, j).start()

                out_copy(m, j).start()
            return carry

        lax.fori_loop(0, windows, window, 0)

        def finish(m, carry):
            for j in range(vchunks):
                mate_copy(m, j).wait_send()
                part_copy(m, j).wait_send()
                out_copy(m, j).wait()

                @pl.when(sec < sec_n - 1)
                def _():
                    section_copy(m, j).wait_send()

            @pl.when(ctx < ctx_n - 1)
            def _():
                for j in range(vchunks + 1):
                    halo_copy(m, j).wait_send()
                for h in range(heads):
                    state_copy(m, h).wait_send()

            return carry

        lax.fori_loop(0, windows, finish, 0)

    return kernel


def local(
    tokens, norm_gain, w_query, w_key, w_value, conv_query, conv_key, conv_value, value_gain, w_out, doc_start, pad_length
):
    windows, span, half = tokens.shape
    width = 2 * half
    rows_n = windows * span
    heads = half // HD
    vchunks = half // CHUNK
    sizes = (lax.axis_size("ctx"), lax.axis_size("section"), windows, span, width, conv_query.shape[1])
    hbm = pl.BlockSpec(memory_space=pltpu.MemorySpace.HBM)
    dma = pltpu.SemaphoreType.DMA
    vmem = pltpu.VMEM
    out = pl.pallas_call(
        make_kernel(sizes),
        out_shape=jax.ShapeDtypeStruct((rows_n, half), BF16),
        in_specs=[hbm] * 12,
        out_specs=hbm,
        scratch_shapes=[
            pltpu.SMEM((windows,), jnp.int32),
            pltpu.SMEM((windows,), jnp.int32),
            vmem(norm_gain.shape, BF16),
            vmem(conv_query.shape, BF16),
            vmem(conv_key.shape, BF16),
            vmem(conv_value.shape, BF16),
            vmem(value_gain.shape, BF16),
            dma((7,)),
            vmem((vchunks + 1, width, CHUNK), BF16),
            vmem((2 * vchunks, half, CHUNK), BF16),
            vmem((windows, 2 * vchunks, span, CHUNK), BF16),
            vmem((2 * vchunks, span, CHUNK), BF16),
            vmem((heads + CHUNK // HD, span + 8, HD), F32),
            vmem((windows, vchunks + 1, 8, HD), F32),
            vmem((windows, vchunks + 1, 8, HD), F32),
            vmem((2, span, 2 * HD), BF16),
            vmem((2, span, 2 * HD), BF16),
            vmem((heads, 2 * FD, span), F32),
            vmem((heads, 2 * FD, span), F32),
            vmem((heads, span, HD), BF16),
            vmem((heads, FROWS, HD), F32),
            vmem((windows, heads, FROWS, HD), BF16),
            vmem((windows, heads, FROWS, HD), BF16),
            vmem((heads, span, FROWS), BF16),
            vmem((heads, span, HD), F32),
            vmem((heads, span, HD), BF16),
            vmem((span, span), BF16),
            vmem((windows, vchunks, span, CHUNK), F32),
            vmem((windows, vchunks, span, CHUNK), F32),
            vmem((windows, vchunks, span, CHUNK), BF16),
            dma((2 + 3 * vchunks,)),
            dma((windows, vchunks)),
            dma((windows, vchunks)),
            dma((windows, vchunks)),
            dma((windows, vchunks)),
            dma((windows, vchunks)),
            dma((windows, vchunks)),
            dma((windows, vchunks + 1)),
            dma((windows, vchunks + 1)),
            dma((windows, heads)),
            dma((windows, heads)),
            dma((windows, vchunks)),
            dma((windows, vchunks)),
        ],
        compiler_params=pltpu.CompilerParams(
            collective_id=0, has_side_effects=True, vmem_limit_bytes=60 * 1024 * 1024
        ),
        name="layers",
    )(
        doc_start, pad_length, tokens.reshape(rows_n, half), norm_gain, w_query, w_key, w_value,
        conv_query, conv_key, conv_value, value_gain, w_out,
    )
    return out.reshape(1, windows, span, half)


def solution(mesh):
    return jax.shard_map(
        local,
        mesh=mesh,
        in_specs=(
            P("groups", "ctx", "head"),
            P("section", None),
            P("section", None, "head"),
            P("section", None, "head"),
            P("section", None, "head"),
            P("section", None, "head"),
            P("section", None, "head"),
            P("section", None, "head"),
            P("section", "head"),
            P("section", "head", None),
            P("groups"),
            P("groups"),
        ),
        out_specs=P("section", "groups", "ctx", "head"),
        check_vma=False,
    )
```

```python
import math

import jax
import jax.numpy as jnp
from jax import lax
from jax.experimental import pallas as pl
from jax.experimental.pallas import tpu as pltpu
from jax.sharding import PartitionSpec as P

HD = 128
FD = 16
FROWS = 160
CHUNK = 256
EPS = 1e-06
MESH = pl.DeviceIdType.MESH
F32 = jnp.float32
BF16 = jnp.bfloat16


def features(doubled, h, lead):
    y = doubled[h, pl.ds(0, FD), :]
    rows = [y, y * y * math.sqrt(0.5)]
    for d in range(1, FD // 2):
        rows.append(y * doubled[h, pl.ds(d, FD), :])
    half = FD // 2
    rows.append(y[:half] * y[half:])
    top = lax.broadcasted_iota(jnp.int32, (half, y.shape[1]), 0) == 0
    rows.append(jnp.where(top, lead, 0.0))
    return jnp.concatenate(rows, axis=0).astype(BF16)


def make_kernel(sizes):
    ctx_n, sec_n, windows, span, width, taps = sizes
    half = width // 2
    heads = half // HD
    vchunks = half // CHUNK
    pair = heads // vchunks
    wide = CHUNK // HD

    def kernel(
        start_in, pad_in, tok_in, gain_in, wq_ref, wk_ref, wv_ref, cq_in, ck_in, cv_in, vg_in, wo_ref,
        out_hbm,
        start_ref, pad_ref, gain_ref, cq_ref, ck_ref, cv_ref, vg_ref, small_sem,
        w_all, wo_v, x_ref, n_ref, pr_ref, ho_ref, hi_ref, q3_ref, k3_ref, qt_ref, kt_ref, v_ref,
        bs_ref, got_ref, fwd_ref, qf_ref, num_ref, mix_ref, mask_ref, part_ref, other_ref, own_ref, o_ref,
        w_sem, tok_sem, out_sem, x_send, x_recv, sec_send, sec_recv, halo_send, halo_recv, st_send, st_recv,
        p_send, p_recv,
    ):
        ctx = lax.axis_index("ctx")
        sec = lax.axis_index("section")
        core = lax.axis_index("head")
        mate = 1 - core
        mine_at = pl.ds(core * vchunks, vchunks)
        mate_at = pl.ds(mate * vchunks, vchunks)

        def cols(j):
            return pl.ds(j * CHUNK, CHUNK)

        def rows(m):
            return pl.ds(pl.multiple_of(m * span, span), span)

        def side(h):
            return pl.ds(pl.multiple_of((h % wide) * HD, HD), HD)

        def tok_load(m, j):
            return pltpu.make_async_copy(
                tok_in.at[rows(m), cols(j)], x_ref.at[m, core * vchunks + j], tok_sem.at[m]
            )

        @pl.when(sec == 0)
        def _():
            for m in range(windows):
                for j in range(vchunks):
                    tok_load(m, j).start()

        small = [
            pltpu.make_async_copy(source, target, small_sem.at[i])
            for i, (source, target) in enumerate(
                (
                    (gain_in, gain_ref),
                    (start_in, start_ref),
                    (pad_in, pad_ref),
                    (cq_in, cq_ref),
                    (ck_in, ck_ref),
                    (cv_in, cv_ref),
                    (vg_in, vg_ref),
                )
            )
        ]
        for load in small:
            load.start()

        pltpu.make_async_copy(wq_ref.at[0], w_all.at[0, :, pl.ds(0, HD)], w_sem.at[0]).start()
        pltpu.make_async_copy(wk_ref.at[0], w_all.at[0, :, pl.ds(HD, HD)], w_sem.at[0]).start()
        for j in range(vchunks):
            pltpu.make_async_copy(wv_ref.at[0, :, cols(j)], w_all.at[1 + j], w_sem.at[1 + j]).start()
        for j in range(2 * vchunks):
            pltpu.make_async_copy(wo_ref.at[0, :, cols(j)], wo_v.at[j], w_sem.at[1 + vchunks]).start()

        def weights_ready(j):
            pltpu.make_async_copy(w_all.at[j], w_all.at[j], w_sem.at[j]).wait()

        barrier = pltpu.get_barrier_semaphore()
        pl.semaphore_signal(barrier, inc=1, device_id={"head": mate}, device_id_type=MESH)

        @pl.when(ctx > 0)
        def _():
            pl.semaphore_signal(barrier, inc=1, device_id={"ctx": ctx - 1}, device_id_type=MESH)

        @pl.when(ctx < ctx_n - 1)
        def _():
            pl.semaphore_signal(barrier, inc=1, device_id={"ctx": ctx + 1}, device_id_type=MESH)

        @pl.when(sec > 0)
        def _():
            pl.semaphore_signal(barrier, inc=1, device_id={"section": sec - 1}, device_id_type=MESH)

        @pl.when(sec < sec_n - 1)
        def _():
            pl.semaphore_signal(barrier, inc=1, device_id={"section": sec + 1}, device_id_type=MESH)

        first = ctx * span
        lead_pos = lax.broadcasted_iota(jnp.int32, (1, span), 1) + first
        col_pos = lax.broadcasted_iota(jnp.int32, (span, HD), 0) + first
        lane = lax.broadcasted_iota(jnp.int32, (1, HD), 1)
        low_half = lane < HD // 2
        lane_head = (lax.broadcasted_iota(jnp.int32, (1, 2 * HD), 1) % (HD // 2)) // FD

        @pl.when(ctx == 0)
        def _():
            for m in range(windows):
                pr_ref[m, :, pl.ds(0, 8), :] = jnp.zeros((heads + wide, 8, HD), F32)

            def clear(i, carry):
                got_ref[i // heads, i % heads] = jnp.zeros((FROWS, HD), BF16)
                return carry

            lax.fori_loop(0, windows * heads, clear, 0)

        peers = (
            1
            + jnp.where(ctx > 0, 1, 0)
            + jnp.where(ctx < ctx_n - 1, 1, 0)
            + jnp.where(sec > 0, 1, 0)
            + jnp.where(sec < sec_n - 1, 1, 0)
        )
        pl.semaphore_wait(barrier, peers)

        def remote(source, target, send, recv, where):
            return pltpu.make_async_remote_copy(
                src_ref=source, dst_ref=target, send_sem=send, recv_sem=recv, device_id=where, device_id_type=MESH
            )

        after_ctx = {"ctx": ctx + 1}

        def section_copy(m, j):
            return remote(
                o_ref.at[m, j], x_ref.at[m, core * vchunks + j], sec_send, sec_recv.at[m, j], {"section": sec + 1}
            )

        def mate_copy(m, j):
            at = x_ref.at[m, core * vchunks + j]
            return remote(at, at, x_send, x_recv.at[m], {"head": mate})

        def mate_wait(m):
            at = x_ref.at[m, mate_at]
            remote(at, at, x_send, x_recv.at[m], {"head": mate}).wait_recv()

        def halo_copy(m, i):
            at = pl.ds(2 * i, 2 if i == 0 else vchunks - 1)
            return remote(ho_ref.at[m, at], hi_ref.at[m, at], halo_send, halo_recv.at[m, i], after_ctx)

        def state_copy(m, h):
            return remote(fwd_ref.at[m, h], got_ref.at[m, h], st_send, st_recv.at[m, h], after_ctx)

        def part_copy(m, j):
            return remote(part_ref.at[m, j], other_ref.at[m, j], p_send, p_recv.at[m, j], {"head": mate})

        def out_copy(m, j):
            return pltpu.make_async_copy(o_ref.at[m, j], out_hbm.at[rows(m), cols(j)], out_sem)

        @pl.when(sec == 0)
        def _():
            for m in range(windows):
                at = x_ref.at[m, mine_at]
                pltpu.make_async_copy(at, at, tok_sem.at[m]).wait()
                for j in range(vchunks):
                    mate_copy(m, j).start()

        def exchange(m):
            @pl.when(sec > 0)
            def _():
                for j in range(vchunks):
                    section_copy(m, j).wait_recv()
                    mate_copy(m, j).start()

        exchange(0)

        for load in small:
            load.wait()

        def normalise(m):
            total = None
            for k in range(2 * vchunks):
                value = x_ref[m, k].astype(F32)
                square = value * value
                for c in range(wide):
                    part = square[:, c * HD : (c + 1) * HD]
                    total = part if total is None else total + part
            scale = lax.rsqrt(jnp.sum(total, axis=1, keepdims=True) * (1.0 / width) + EPS)
            for k in range(2 * vchunks):
                gain = gain_ref[:, cols(k)].astype(F32)
                n_ref[m, k] = (x_ref[m, k].astype(F32) * scale * gain).astype(BF16)

        def project(ms, j):
            rows_in = jnp.concatenate(
                [jnp.concatenate([n_ref[m, k] for k in range(2 * vchunks)], axis=1) for m in ms], axis=0
            )
            got = jnp.dot(rows_in, w_all[j], preferred_element_type=F32).astype(BF16).astype(F32)
            for i, m in enumerate(ms):
                for c in range(wide):
                    own = got[i * span : (i + 1) * span, c * HD : (c + 1) * HD]
                    pr_ref[m, wide * j + c, pl.ds(8, span), :] = own
                    ho_ref[m, j, pl.ds(4 * c, 4), :] = own[span - 4 :]

        def halo_send_off(m, i):
            @pl.when(ctx < ctx_n - 1)
            def _():
                halo_copy(m, i).start()

        def halo_wait(m, i):
            @pl.when(ctx > 0)
            def _():
                halo_copy(m, i).wait_recv()
                for j in range(2) if i == 0 else range(2, vchunks + 1):
                    for c in range(wide):
                        pr_ref[m, wide * j + c, pl.ds(4, 4), :] = hi_ref[m, j, pl.ds(4 * c, 4), :]

        def conv(m, c, taps_ref, tap_at, since):
            total = taps_ref[0, pl.ds(0, 1), tap_at].astype(F32) * pr_ref[m, c, pl.ds(8, span), :]
            for j in range(1, taps):
                term = taps_ref[0, pl.ds(j, 1), tap_at].astype(F32) * pr_ref[m, c, pl.ds(8 - j, span), :]
                total = total + jnp.where(since >= j, term, 0.0)
            return total

        def inside(m):
            return jnp.logical_and(start_ref[m] >= first, start_ref[m] < first + span)

        def arrive(m):
            start = start_ref[m]
            since = col_pos - start
            since = jnp.where(since < 0, taps, since)
            kept = jnp.where(jnp.logical_or(lead_pos >= start, jnp.logical_not(inside(m))), 1.0, 0.0)
            used = jnp.where(jnp.logical_or(lead_pos < start, start < first), 1.0, 0.0)

            def conv_query_key():
                for which, taps_ref, wide_ref, turned_ref, lead in (
                    (1, ck_ref, k3_ref, kt_ref, kept),
                    (0, cq_ref, q3_ref, qt_ref, used),
                ):
                    part = conv(m, which, taps_ref, pl.ds(0, HD), since)
                    turned = jnp.transpose(part) * (0.5 * lead)
                    for h in range(heads):
                        own = turned[h * FD : (h + 1) * FD]
                        turned_ref[h, pl.ds(0, FD), :] = own
                        turned_ref[h, pl.ds(FD, FD), :] = own
                    if which == 0:
                        part = part * (1.0 / math.sqrt(FD))
                    rolled = pltpu.roll(part, HD // 2, 1)
                    for g in range(2):
                        both = jnp.where(low_half, part, rolled) if g == 0 else jnp.where(low_half, rolled, part)
                        high = both.astype(BF16).astype(F32)
                        low = both - high
                        if which == 0:
                            wide_ref[g, :, pl.ds(0, HD)] = high.astype(BF16)
                            wide_ref[g, :, pl.ds(HD, HD)] = low.astype(BF16)
                        else:
                            wide_ref[g, :, pl.ds(0, HD)] = jnp.where(low_half, high, low).astype(BF16)
                            wide_ref[g, :, pl.ds(HD, HD)] = jnp.where(low_half, high, 0.0).astype(BF16)

            def values(h):
                at = pl.ds((h % wide) * HD, HD)
                v_ref[h // wide, :, at] = conv(m, wide + h, cv_ref, pl.ds(h * HD, HD), since).astype(BF16)
                made = jnp.dot(features(kt_ref, h, kept), v_ref[h // wide, :, at], preferred_element_type=F32)
                fwd_ref[m, h] = made.astype(BF16)
                bs_ref[m, h] = made

            def send_states(low, high):
                if ctx_n > 1:

                    @pl.when(ctx == 0)
                    def _():
                        for h in range(low, high):
                            state_copy(m, h).start()

            mate_wait(m)
            normalise(m)

            @pl.when(m == 0)
            def _():
                weights_ready(0)
                weights_ready(1)

            project([m], 0)
            project([m], 1)
            halo_send_off(m, 0)

            @pl.when(m == 0)
            def _():
                for j in range(2, vchunks + 1):
                    weights_ready(j)

            for j in range(2, vchunks + 1):
                project([m], j)
            halo_send_off(m, 1)
            halo_wait(m, 0)
            halo_wait(m, 1)
            conv_query_key()
            for h in range(heads // 2):
                values(h)
            send_states(0, heads // 2)
            for h in range(heads // 2, heads):
                values(h)

            edge = start - first
            row_pos = lax.broadcasted_iota(jnp.int32, (span, span), 0)
            other_pos = lax.broadcasted_iota(jnp.int32, (span, span), 1)
            allowed = jnp.logical_and(other_pos <= row_pos, (other_pos >= edge) == (row_pos >= edge))
            mask_ref[...] = jnp.where(allowed, 1.0, 0.0).astype(BF16)

            for g in range(2):
                stacked = jnp.concatenate(
                    [jnp.where(lane_head == c, q3_ref[g], jnp.zeros((), BF16)) for c in range(heads // 2)], axis=0
                )
                s_all = lax.dot_general(stacked, k3_ref[g], (((1,), (1,)), ((), ())), preferred_element_type=F32)
                for c in range(heads // 2):
                    h = g * (heads // 2) + c
                    s = s_all[c * span : (c + 1) * span]
                    weight = ((0.5 * s + 1.0) * s + 1.0).astype(BF16) * mask_ref[...]
                    num_ref[m, h] = jnp.dot(
                        weight, v_ref[h // wide, :, pl.ds((h % wide) * HD, HD)], preferred_element_type=F32
                    )
                    qf_ref[m, h] = jnp.transpose(features(qt_ref, h, used))
            send_states(heads // 2, heads)

        def states_pass(m):
            reset = inside(m)

            def chain(h, carry):
                @pl.when(ctx > 0)
                def _():
                    state_copy(m, h).wait_recv()

                @pl.when(jnp.logical_and(ctx > 0, ctx < ctx_n - 1))
                def _():
                    old = got_ref[m, h].astype(F32)
                    fwd_ref[m, h] = (bs_ref[m, h] + jnp.where(reset, 0.0, old)).astype(BF16)
                    state_copy(m, h).start()

                num = num_ref[m, h] + jnp.dot(qf_ref[m, h], got_ref[m, h], preferred_element_type=F32)
                square = jnp.mean(num * num, axis=1, keepdims=True)
                mix_ref[h // wide, :, side(h)] = (
                    num * lax.rsqrt(square + EPS) * vg_ref[:, pl.ds(pl.multiple_of(h * HD, HD), HD)].astype(F32)
                ).astype(BF16)
                return carry

            lax.fori_loop(0, heads, chain, 0)

        def output(m):
            @pl.when(m == 0)
            def _():
                pltpu.make_async_copy(wo_v, wo_v, w_sem.at[1 + vchunks]).wait()

            def mixed():
                return jnp.concatenate([mix_ref[k] for k in range(vchunks)], axis=1)

            for j in range(vchunks):
                part_ref[m, j] = jnp.dot(mixed(), wo_v[mate * vchunks + j], preferred_element_type=F32)
            for j in range(vchunks):
                part_copy(m, j).start()
            for j in range(vchunks):
                own_ref[j] = jnp.dot(mixed(), wo_v[core * vchunks + j], preferred_element_type=F32)
            valid = first + lax.broadcasted_iota(jnp.int32, (span, CHUNK), 0) < span * ctx_n - pad_ref[m]
            for j in range(vchunks):
                part_copy(m, j).wait_recv()
                update = jnp.where(valid, own_ref[j] + other_ref[m, j], 0.0)
                o_ref[m, j] = (x_ref[m, core * vchunks + j].astype(F32) + update).astype(BF16)

                @pl.when(sec < sec_n - 1)
                def _():
                    section_copy(m, j).start()

                out_copy(m, j).start()

        def step(t, carry):
            def slot(u, carry):
                @pl.when(jnp.logical_and(u == 1, t < windows))
                def _():
                    arrive(t)

                @pl.when(jnp.logical_and(u == 0, t > 0))
                def _():
                    @pl.when(t < windows)
                    def _():
                        exchange(t)

                    output(t - 1)

                return carry

            lax.fori_loop(0, 2, slot, 0)

            @pl.when(t < windows)
            def _():
                states_pass(t)

            return carry

        lax.fori_loop(0, windows + 1, step, 0)

        def sent(ref, sem):
            remote(ref, ref, sem, sem, {"head": mate}).wait_send()

        sent(x_ref.at[:, mine_at], x_send)
        sent(part_ref, p_send)
        sent(o_ref, out_sem)

        @pl.when(sec < sec_n - 1)
        def _():
            sent(o_ref, sec_send)

        @pl.when(ctx < ctx_n - 1)
        def _():
            sent(ho_ref, halo_send)
            sent(fwd_ref, st_send)

    return kernel


def local(
    tokens, norm_gain, w_query, w_key, w_value, conv_query, conv_key, conv_value, value_gain, w_out, doc_start, pad_length
):
    windows, span, half = tokens.shape
    width = 2 * half
    rows_n = windows * span
    heads = half // HD
    vchunks = half // CHUNK
    sizes = (lax.axis_size("ctx"), lax.axis_size("section"), windows, span, width, conv_query.shape[1])
    hbm = pl.BlockSpec(memory_space=pltpu.MemorySpace.HBM)
    dma = pltpu.SemaphoreType.DMA
    vmem = pltpu.VMEM
    out = pl.pallas_call(
        make_kernel(sizes),
        out_shape=pltpu.VMEM((rows_n, half), BF16),
        in_specs=[hbm] * 12,
        out_specs=pl.BlockSpec(memory_space=pltpu.VMEM),
        scratch_shapes=[
            pltpu.SMEM((windows,), jnp.int32),
            pltpu.SMEM((windows,), jnp.int32),
            vmem(norm_gain.shape, BF16),
            vmem(conv_query.shape, BF16),
            vmem(conv_key.shape, BF16),
            vmem(conv_value.shape, BF16),
            vmem(value_gain.shape, BF16),
            dma((7,)),
            vmem((vchunks + 1, width, CHUNK), BF16),
            vmem((2 * vchunks, half, CHUNK), BF16),
            vmem((windows, 2 * vchunks, span, CHUNK), BF16),
            vmem((windows, 2 * vchunks, span, CHUNK), BF16),
            vmem((windows, heads + CHUNK // HD, span + 8, HD), F32),
            vmem((windows, vchunks + 1, 8, HD), F32),
            vmem((windows, vchunks + 1, 8, HD), F32),
            vmem((2, span, 2 * HD), BF16),
            vmem((2, span, 2 * HD), BF16),
            vmem((heads, 2 * FD, span), F32),
            vmem((heads, 2 * FD, span), F32),
            vmem((vchunks, span, CHUNK), BF16),
            vmem((windows, heads, FROWS, HD), F32),
            vmem((windows, heads, FROWS, HD), BF16),
            vmem((windows, heads, FROWS, HD), BF16),
            vmem((windows, heads, span, FROWS), BF16),
            vmem((windows, heads, span, HD), F32),
            vmem((vchunks, span, CHUNK), BF16),
            vmem((span, span), BF16),
            vmem((windows, vchunks, span, CHUNK), F32),
            vmem((windows, vchunks, span, CHUNK), F32),
            vmem((vchunks, span, CHUNK), F32),
            vmem((windows, vchunks, span, CHUNK), BF16),
            dma((2 + vchunks,)),
            dma((windows,)),
            dma(()),
            dma(()),
            dma((windows,)),
            dma(()),
            dma((windows, vchunks)),
            dma(()),
            dma((windows, 2)),
            dma(()),
            dma((windows, heads)),
            dma(()),
            dma((windows, vchunks)),
        ],
        compiler_params=pltpu.CompilerParams(
            collective_id=0, has_side_effects=True, vmem_limit_bytes=60 * 1024 * 1024
        ),
        name="layers",
    )(
        doc_start, pad_length, tokens.reshape(rows_n, half), norm_gain, w_query, w_key, w_value,
        conv_query, conv_key, conv_value, value_gain, w_out,
    )
    return out.reshape(1, windows, span, half)


def solution(mesh):
    return jax.shard_map(
        local,
        mesh=mesh,
        in_specs=(
            P("groups", "ctx", "head"),
            P("section", None),
            P("section", None, "head"),
            P("section", None, "head"),
            P("section", None, "head"),
            P("section", None, "head"),
            P("section", None, "head"),
            P("section", None, "head"),
            P("section", "head"),
            P("section", "head", None),
            P("groups"),
            P("groups"),
        ),
        out_specs=P("section", "groups", "ctx", "head"),
        check_vma=False,
    )
```

```python
import math

import jax
import jax.numpy as jnp
from jax import lax
from jax.experimental import pallas as pl
from jax.experimental.pallas import tpu as pltpu
from jax.sharding import PartitionSpec as P

HD = 128
FD = 16
FROWS = 160
PIECES = 2
CHUNK = 256
EPS = 1e-06
MESH = pl.DeviceIdType.MESH
F32 = jnp.float32
BF16 = jnp.bfloat16


def features(doubled, h, lead):
    y = doubled[h, pl.ds(0, FD), :]
    rows = [y, y * y * math.sqrt(0.5)]
    for d in range(1, FD // 2):
        rows.append(y * doubled[h, pl.ds(d, FD), :])
    half = FD // 2
    rows.append(y[:half] * y[half:])
    top = lax.broadcasted_iota(jnp.int32, (half, y.shape[1]), 0) == 0
    rows.append(jnp.where(top, lead, 0.0))
    return jnp.concatenate(rows, axis=0).astype(BF16)


def make_kernel(sizes):
    ctx_n, sec_n, windows, span, width, taps = sizes
    half = width // 2
    heads = half // HD
    vchunks = half // CHUNK
    pair = heads // vchunks
    wide = CHUNK // HD

    def kernel(
        start_in, pad_in, tok_in, gain_in, wq_ref, wk_ref, wv_ref, cq_in, ck_in, cv_in, vg_in, wo_ref,
        out_ref,
        start_ref, pad_ref, gain_ref, cq_ref, ck_ref, cv_ref, vg_ref, small_sem,
        w_all, wo_v, x_ref, n_ref, pr_ref, ho_ref, hi_ref, q3_ref, k3_ref, qt_ref, kt_ref, v_ref,
        bs_ref, got_ref, fwd_ref, qf_ref, num_ref, mix_ref, mask_ref, part_ref, other_ref, own_ref,
        w_sem, tok_sem, x_send, x_recv, sec_send, sec_recv, halo_send, halo_recv, st_send, st_recv,
        p_send, p_recv,
    ):
        ctx = lax.axis_index("ctx")
        sec = lax.axis_index("section")
        core = lax.axis_index("head")
        mate = 1 - core
        mine_at = pl.ds(core * vchunks, vchunks)
        mate_at = pl.ds(mate * vchunks, vchunks)

        def cols(j):
            return pl.ds(j * CHUNK, CHUNK)

        def rows(m):
            return pl.ds(pl.multiple_of(m * span, span), span)

        def tok_load(m, j):
            return pltpu.make_async_copy(
                tok_in.at[rows(m), cols(j)], x_ref.at[m, core * vchunks + j], tok_sem.at[m]
            )

        @pl.when(sec == 0)
        def _():
            for m in range(windows):
                for j in range(vchunks):
                    tok_load(m, j).start()

        small = [
            pltpu.make_async_copy(source, target, small_sem.at[i])
            for i, (source, target) in enumerate(
                (
                    (gain_in, gain_ref),
                    (start_in, start_ref),
                    (pad_in, pad_ref),
                    (cq_in, cq_ref),
                    (ck_in, ck_ref),
                    (cv_in, cv_ref),
                    (vg_in, vg_ref),
                )
            )
        ]
        for load in small:
            load.start()

        pltpu.make_async_copy(wq_ref.at[0], w_all.at[0, :, pl.ds(0, HD)], w_sem.at[0]).start()
        pltpu.make_async_copy(wk_ref.at[0], w_all.at[0, :, pl.ds(HD, HD)], w_sem.at[0]).start()
        for j in range(vchunks):
            pltpu.make_async_copy(wv_ref.at[0, :, cols(j)], w_all.at[1 + j], w_sem.at[1 + j]).start()
        for j in range(2 * vchunks):
            pltpu.make_async_copy(wo_ref.at[0, :, cols(j)], wo_v.at[j], w_sem.at[1 + vchunks]).start()

        def weights_ready(j):
            pltpu.make_async_copy(w_all.at[j], w_all.at[j], w_sem.at[j]).wait()

        barrier = pltpu.get_barrier_semaphore()
        pl.semaphore_signal(barrier, inc=1, device_id={"head": mate}, device_id_type=MESH)

        @pl.when(ctx > 0)
        def _():
            pl.semaphore_signal(barrier, inc=1, device_id={"ctx": ctx - 1}, device_id_type=MESH)

        @pl.when(ctx < ctx_n - 1)
        def _():
            pl.semaphore_signal(barrier, inc=1, device_id={"ctx": ctx + 1}, device_id_type=MESH)

        @pl.when(sec > 0)
        def _():
            pl.semaphore_signal(barrier, inc=1, device_id={"section": sec - 1}, device_id_type=MESH)

        @pl.when(sec < sec_n - 1)
        def _():
            pl.semaphore_signal(barrier, inc=1, device_id={"section": sec + 1}, device_id_type=MESH)

        first = ctx * span
        lead_pos = lax.broadcasted_iota(jnp.int32, (1, span), 1) + first
        col_pos = lax.broadcasted_iota(jnp.int32, (span, HD), 0) + first
        lane = lax.broadcasted_iota(jnp.int32, (1, HD), 1)
        low_half = lane < HD // 2
        lane_head = (lax.broadcasted_iota(jnp.int32, (1, 2 * HD), 1) % (HD // 2)) // FD

        @pl.when(ctx == 0)
        def _():
            for m in range(windows):
                pr_ref[m, :, pl.ds(0, 8), :] = jnp.zeros((heads + wide, 8, HD), F32)

            def clear(i, carry):
                got_ref[i // heads, i % heads] = jnp.zeros((FROWS, HD), BF16)
                return carry

            lax.fori_loop(0, windows * heads, clear, 0)

        peers = (
            1
            + jnp.where(ctx > 0, 1, 0)
            + jnp.where(ctx < ctx_n - 1, 1, 0)
            + jnp.where(sec > 0, 1, 0)
            + jnp.where(sec < sec_n - 1, 1, 0)
        )
        pl.semaphore_wait(barrier, peers)

        def remote(source, target, send, recv, where):
            return pltpu.make_async_remote_copy(
                src_ref=source, dst_ref=target, send_sem=send, recv_sem=recv, device_id=where, device_id_type=MESH
            )

        after_ctx = {"ctx": ctx + 1}

        def section_copy(m, j):
            return remote(
                out_ref.at[rows(m), cols(j)], x_ref.at[m, core * vchunks + j], sec_send, sec_recv.at[m, j], {"section": sec + 1}
            )

        def mate_copy(m, j):
            at = x_ref.at[m, core * vchunks + j]
            return remote(at, at, x_send, x_recv.at[m], {"head": mate})

        def mate_wait(m):
            at = x_ref.at[m, mate_at]
            remote(at, at, x_send, x_recv.at[m], {"head": mate}).wait_recv()

        def halo_copy(m, i):
            at = pl.ds(2 * i, 2 if i == 0 else vchunks - 1)
            return remote(ho_ref.at[m, at], hi_ref.at[m, at], halo_send, halo_recv.at[m, i], after_ctx)

        def piece(p):
            return pl.ds(pl.multiple_of(p * (FROWS // PIECES), FROWS // PIECES), FROWS // PIECES)

        def state_copy(m, h, p):
            return remote(
                fwd_ref.at[m, h, piece(p)], got_ref.at[m, h, piece(p)], st_send, st_recv.at[m, h, p], after_ctx
            )

        def part_copy(m, j):
            return remote(part_ref.at[m, j], other_ref.at[m, j], p_send, p_recv.at[m, j], {"head": mate})

        @pl.when(sec == 0)
        def _():
            for m in range(windows):
                at = x_ref.at[m, mine_at]
                pltpu.make_async_copy(at, at, tok_sem.at[m]).wait()
                for j in range(vchunks):
                    mate_copy(m, j).start()

        def exchange(m):
            @pl.when(sec > 0)
            def _():
                for j in range(vchunks):
                    section_copy(m, j).wait_recv()
                    mate_copy(m, j).start()

        for load in small:
            load.wait()

        def normalise(m):
            total = None
            for k in range(2 * vchunks):
                value = x_ref[m, k].astype(F32)
                square = value * value
                for c in range(wide):
                    part = square[:, c * HD : (c + 1) * HD]
                    total = part if total is None else total + part
            scale = lax.rsqrt(jnp.sum(total, axis=1, keepdims=True) * (1.0 / width) + EPS)
            for k in range(2 * vchunks):
                gain = gain_ref[:, cols(k)].astype(F32)
                n_ref[m, k] = (x_ref[m, k].astype(F32) * scale * gain).astype(BF16)

        def project(ms, j):
            rows_in = jnp.concatenate(
                [jnp.concatenate([n_ref[m, k] for k in range(2 * vchunks)], axis=1) for m in ms], axis=0
            )
            got = jnp.dot(rows_in, w_all[j], preferred_element_type=F32).astype(BF16).astype(F32)
            for i, m in enumerate(ms):
                for c in range(wide):
                    own = got[i * span : (i + 1) * span, c * HD : (c + 1) * HD]
                    pr_ref[m, wide * j + c, pl.ds(8, span), :] = own
                    ho_ref[m, j, pl.ds(4 * c, 4), :] = own[span - 4 :]

        def halo_send_off(m, i):
            @pl.when(ctx < ctx_n - 1)
            def _():
                halo_copy(m, i).start()

        def halo_wait(m, i):
            @pl.when(ctx > 0)
            def _():
                halo_copy(m, i).wait_recv()
                for j in range(2) if i == 0 else range(2, vchunks + 1):
                    for c in range(wide):
                        pr_ref[m, wide * j + c, pl.ds(4, 4), :] = hi_ref[m, j, pl.ds(4 * c, 4), :]

        def conv(m, c, taps_ref, tap_at, since):
            total = taps_ref[0, pl.ds(0, 1), tap_at].astype(F32) * pr_ref[m, c, pl.ds(8, span), :]
            for j in range(1, taps):
                term = taps_ref[0, pl.ds(j, 1), tap_at].astype(F32) * pr_ref[m, c, pl.ds(8 - j, span), :]
                total = total + jnp.where(since >= j, term, 0.0)
            return total

        def prepare(m):
            mate_wait(m)
            normalise(m)

            @pl.when(m == 0)
            def _():
                weights_ready(0)
                weights_ready(1)

            project([m], 0)
            project([m], 1)
            halo_send_off(m, 0)

            @pl.when(m == 0)
            def _():
                for j in range(2, vchunks + 1):
                    weights_ready(j)

            for j in range(2, vchunks + 1):
                project([m], j)
            halo_send_off(m, 1)

        def inside(m):
            return jnp.logical_and(start_ref[m] >= first, start_ref[m] < first + span)

        def used_of(m):
            return jnp.where(jnp.logical_or(lead_pos < start_ref[m], start_ref[m] < first), 1.0, 0.0)

        def arrive(m):
            start = start_ref[m]
            since = col_pos - start
            since = jnp.where(since < 0, taps, since)
            kept = jnp.where(jnp.logical_or(lead_pos >= start, jnp.logical_not(inside(m))), 1.0, 0.0)
            used = used_of(m)

            def conv_query_key():
                for which, taps_ref, wide_ref, turned_ref, lead in (
                    (1, ck_ref, k3_ref, kt_ref, kept),
                    (0, cq_ref, q3_ref, qt_ref, used),
                ):
                    part = conv(m, which, taps_ref, pl.ds(0, HD), since)
                    turned = jnp.transpose(part) * (0.5 * lead)
                    for h in range(heads):
                        own = turned[h * FD : (h + 1) * FD]
                        turned_ref[h, pl.ds(0, FD), :] = own
                        turned_ref[h, pl.ds(FD, FD), :] = own
                    if which == 0:
                        part = part * (1.0 / math.sqrt(FD))
                    rolled = pltpu.roll(part, HD // 2, 1)
                    for g in range(2):
                        both = jnp.where(low_half, part, rolled) if g == 0 else jnp.where(low_half, rolled, part)
                        high = both.astype(BF16).astype(F32)
                        low = both - high
                        if which == 0:
                            wide_ref[g, :, pl.ds(0, HD)] = high.astype(BF16)
                            wide_ref[g, :, pl.ds(HD, HD)] = low.astype(BF16)
                        else:
                            wide_ref[g, :, pl.ds(0, HD)] = jnp.where(low_half, high, low).astype(BF16)
                            wide_ref[g, :, pl.ds(HD, HD)] = jnp.where(low_half, high, 0.0).astype(BF16)

            def values(h):
                at = pl.ds((h % wide) * HD, HD)
                v_ref[h // wide, :, at] = conv(m, wide + h, cv_ref, pl.ds(h * HD, HD), since).astype(BF16)
                made = jnp.dot(features(kt_ref, h, kept), v_ref[h // wide, :, at], preferred_element_type=F32)
                fwd_ref[m, h] = made.astype(BF16)
                bs_ref[m, h] = made

            def send_states(low, high):
                if ctx_n > 1:

                    @pl.when(ctx == 0)
                    def _():
                        for h in range(low, high):
                            for p in range(PIECES):
                                state_copy(m, h, p).start()

            halo_wait(m, 0)
            halo_wait(m, 1)
            conv_query_key()
            for h in range(heads // 2):
                values(h)
            send_states(0, heads // 2)
            for h in range(heads // 2, heads):
                values(h)
            send_states(heads // 2, heads)

        def within(m):
            start = start_ref[m]
            used = used_of(m)
            edge = start - first
            row_pos = lax.broadcasted_iota(jnp.int32, (span, span), 0)
            other_pos = lax.broadcasted_iota(jnp.int32, (span, span), 1)
            allowed = jnp.logical_and(other_pos <= row_pos, (other_pos >= edge) == (row_pos >= edge))
            mask_ref[...] = jnp.where(allowed, 1.0, 0.0).astype(BF16)

            for g in range(2):
                stacked = jnp.concatenate(
                    [jnp.where(lane_head == c, q3_ref[g], jnp.zeros((), BF16)) for c in range(heads // 2)], axis=0
                )
                s_all = lax.dot_general(stacked, k3_ref[g], (((1,), (1,)), ((), ())), preferred_element_type=F32)
                for c in range(heads // 2):
                    h = g * (heads // 2) + c
                    s = s_all[c * span : (c + 1) * span]
                    weight = ((0.5 * s + 1.0) * s + 1.0).astype(BF16) * mask_ref[...]
                    num_ref[m, h] = jnp.dot(
                        weight, v_ref[h // wide, :, pl.ds((h % wide) * HD, HD)], preferred_element_type=F32
                    )
                    qf_ref[m, h] = jnp.transpose(features(qt_ref, h, used))

        def states_pass(m):
            reset = inside(m)

            def chain(i, carry):
                h, p = i // PIECES, i % PIECES

                @pl.when(ctx > 0)
                def _():
                    state_copy(m, h, p).wait_recv()

                @pl.when(jnp.logical_and(ctx > 0, ctx < ctx_n - 1))
                def _():
                    old = got_ref[m, h, piece(p), :].astype(F32)
                    fwd_ref[m, h, piece(p), :] = (bs_ref[m, h, piece(p), :] + jnp.where(reset, 0.0, old)).astype(BF16)
                    state_copy(m, h, p).start()

                return carry

            lax.fori_loop(0, heads * PIECES, chain, 0)

        def mix(m):
            for h in range(heads):
                num = num_ref[m, h] + jnp.dot(qf_ref[m, h], got_ref[m, h], preferred_element_type=F32)
                square = jnp.mean(num * num, axis=1, keepdims=True)
                mix_ref[h // wide, :, pl.ds((h % wide) * HD, HD)] = (
                    num * lax.rsqrt(square + EPS) * vg_ref[:, pl.ds(h * HD, HD)].astype(F32)
                ).astype(BF16)

        def output(m):
            @pl.when(m == 0)
            def _():
                pltpu.make_async_copy(wo_v, wo_v, w_sem.at[1 + vchunks]).wait()

            def mixed():
                return jnp.concatenate([mix_ref[k] for k in range(vchunks)], axis=1)

            for j in range(vchunks):
                part_ref[m, j] = jnp.dot(mixed(), wo_v[mate * vchunks + j], preferred_element_type=F32).astype(BF16)
            for j in range(vchunks):
                part_copy(m, j).start()
            for j in range(vchunks):
                own_ref[j] = jnp.dot(mixed(), wo_v[core * vchunks + j], preferred_element_type=F32)
            valid = first + lax.broadcasted_iota(jnp.int32, (span, CHUNK), 0) < span * ctx_n - pad_ref[m]
            for j in range(vchunks):
                part_copy(m, j).wait_recv()
                update = jnp.where(valid, own_ref[j] + other_ref[m, j].astype(F32), 0.0)
                out_ref[rows(m), cols(j)] = (x_ref[m, core * vchunks + j].astype(F32) + update).astype(BF16)

                @pl.when(sec < sec_n - 1)
                def _():
                    section_copy(m, j).start()


        last = ctx == ctx_n - 1
        out_turn = jnp.where(sec == 0, 0, jnp.where(last, 1, 2))
        local_turn = jnp.where(last, 0, 0)

        def step(t, carry):
            here = t < windows

            def turn(u, carry):
                @pl.when(jnp.logical_and(u == out_turn, t > 0))
                def _():
                    output(t - 1)

                @pl.when(jnp.logical_and(u == 0, here))
                def _():
                    exchange(t)

                    def slot(v, carry):
                        now = jnp.logical_and(v == 0, jnp.logical_or(sec > 0, t == 0))
                        ahead = jnp.logical_and(v == 1, sec == 0)

                        @pl.when(jnp.logical_and(jnp.logical_or(now, ahead), t + v < windows))
                        def _():
                            prepare(t + v)

                        @pl.when(v == 0)
                        def _():
                            arrive(t)

                        return carry

                    lax.fori_loop(0, 2, slot, 0)

                @pl.when(jnp.logical_and(u == local_turn, here))
                def _():
                    within(t)

                @pl.when(jnp.logical_and(u == 1, here))
                def _():
                    states_pass(t)

                @pl.when(jnp.logical_and(u == 2, here))
                def _():
                    mix(t)

                return carry

            lax.fori_loop(0, 3, turn, 0)
            return carry

        lax.fori_loop(0, windows + 1, step, 0)

        def sent(ref, sem):
            remote(ref, ref, sem, sem, {"head": mate}).wait_send()

        sent(x_ref.at[:, mine_at], x_send)
        sent(part_ref, p_send)

        @pl.when(sec < sec_n - 1)
        def _():
            sent(out_ref, sec_send)

        @pl.when(ctx < ctx_n - 1)
        def _():
            sent(ho_ref, halo_send)
            sent(fwd_ref, st_send)

    return kernel


def local(
    tokens, norm_gain, w_query, w_key, w_value, conv_query, conv_key, conv_value, value_gain, w_out, doc_start, pad_length
):
    windows, span, half = tokens.shape
    width = 2 * half
    rows_n = windows * span
    heads = half // HD
    vchunks = half // CHUNK
    sizes = (lax.axis_size("ctx"), lax.axis_size("section"), windows, span, width, conv_query.shape[1])
    hbm = pl.BlockSpec(memory_space=pltpu.MemorySpace.HBM)
    dma = pltpu.SemaphoreType.DMA
    vmem = pltpu.VMEM
    out = pl.pallas_call(
        make_kernel(sizes),
        out_shape=pltpu.VMEM((rows_n, half), BF16),
        in_specs=[hbm] * 12,
        out_specs=pl.BlockSpec(memory_space=pltpu.VMEM),
        scratch_shapes=[
            pltpu.SMEM((windows,), jnp.int32),
            pltpu.SMEM((windows,), jnp.int32),
            vmem(norm_gain.shape, BF16),
            vmem(conv_query.shape, BF16),
            vmem(conv_key.shape, BF16),
            vmem(conv_value.shape, BF16),
            vmem(value_gain.shape, BF16),
            dma((7,)),
            vmem((vchunks + 1, width, CHUNK), BF16),
            vmem((2 * vchunks, half, CHUNK), BF16),
            vmem((windows, 2 * vchunks, span, CHUNK), BF16),
            vmem((windows, 2 * vchunks, span, CHUNK), BF16),
            vmem((windows, heads + CHUNK // HD, span + 8, HD), F32),
            vmem((windows, vchunks + 1, 8, HD), F32),
            vmem((windows, vchunks + 1, 8, HD), F32),
            vmem((2, span, 2 * HD), BF16),
            vmem((2, span, 2 * HD), BF16),
            vmem((heads, 2 * FD, span), F32),
            vmem((heads, 2 * FD, span), F32),
            vmem((vchunks, span, CHUNK), BF16),
            vmem((windows, heads, FROWS, HD), F32),
            vmem((windows, heads, FROWS, HD), BF16),
            vmem((windows, heads, FROWS, HD), BF16),
            vmem((windows, heads, span, FROWS), BF16),
            vmem((windows, heads, span, HD), F32),
            vmem((vchunks, span, CHUNK), BF16),
            vmem((span, span), BF16),
            vmem((windows, vchunks, span, CHUNK), BF16),
            vmem((windows, vchunks, span, CHUNK), BF16),
            vmem((vchunks, span, CHUNK), F32),
            dma((2 + vchunks,)),
            dma((windows,)),
            dma(()),
            dma((windows,)),
            dma(()),
            dma((windows, vchunks)),
            dma(()),
            dma((windows, 2)),
            dma(()),
            dma((windows, heads, PIECES)),
            dma(()),
            dma((windows, vchunks)),
        ],
        compiler_params=pltpu.CompilerParams(
            collective_id=0, has_side_effects=True, vmem_limit_bytes=60 * 1024 * 1024
        ),
        name="layers",
    )(
        doc_start, pad_length, tokens.reshape(rows_n, half), norm_gain, w_query, w_key, w_value,
        conv_query, conv_key, conv_value, value_gain, w_out,
    )
    return out.reshape(1, windows, span, half)


def solution(mesh):
    return jax.shard_map(
        local,
        mesh=mesh,
        in_specs=(
            P("groups", "ctx", "head"),
            P("section", None),
            P("section", None, "head"),
            P("section", None, "head"),
            P("section", None, "head"),
            P("section", None, "head"),
            P("section", None, "head"),
            P("section", None, "head"),
            P("section", "head"),
            P("section", "head", None),
            P("groups"),
            P("groups"),
        ),
        out_specs=P("section", "groups", "ctx", "head"),
        check_vma=False,
    )
```

```python
import math

import jax
import jax.numpy as jnp
from jax import lax
from jax.experimental import pallas as pl
from jax.experimental.pallas import tpu as pltpu
from jax.sharding import PartitionSpec as P

HD = 128
FD = 16
FROWS = 160
PIECES = 2
CHUNK = 256
EPS = 1e-06
MESH = pl.DeviceIdType.MESH
F32 = jnp.float32
BF16 = jnp.bfloat16


def features(doubled, h, lead):
    y = doubled[h, pl.ds(0, FD), :]
    rows = [y, y * y * math.sqrt(0.5)]
    for d in range(1, FD // 2):
        rows.append(y * doubled[h, pl.ds(d, FD), :])
    half = FD // 2
    rows.append(y[:half] * y[half:])
    top = lax.broadcasted_iota(jnp.int32, (half, y.shape[1]), 0) == 0
    rows.append(jnp.where(top, lead, 0.0))
    return jnp.concatenate(rows, axis=0).astype(BF16)


def make_kernel(sizes):
    ctx_n, sec_n, windows, span, width, taps = sizes
    half = width // 2
    heads = half // HD
    vchunks = half // CHUNK
    pair = heads // vchunks
    wide = CHUNK // HD

    def kernel(
        start_in, pad_in, tok_in, gain_in, wq_ref, wk_ref, wv_ref, cq_in, ck_in, cv_in, vg_in, wo_ref,
        out_ref,
        start_ref, pad_ref, gain_ref, cq_ref, ck_ref, cv_ref, vg_ref, small_sem,
        w_all, wo_v, x_ref, n_ref, pr_ref, ho_ref, hi_ref, q3_ref, k3_ref, qt_ref, kt_ref, v_ref,
        bs_ref, got_ref, fwd_ref, qf_ref, num_ref, mix_ref, mask_ref, part_ref, other_ref, own_ref,
        w_sem, tok_sem, x_send, x_recv, sec_send, sec_recv, halo_send, halo_recv, st_send, st_recv,
        p_send, p_recv,
    ):
        ctx = lax.axis_index("ctx")
        sec = lax.axis_index("section")
        core = lax.axis_index("head")
        mate = 1 - core
        mine_at = pl.ds(core * vchunks, vchunks)
        mate_at = pl.ds(mate * vchunks, vchunks)

        def cols(j):
            return pl.ds(j * CHUNK, CHUNK)

        def rows(m):
            return pl.ds(pl.multiple_of(m * span, span), span)

        def tok_load(m, j):
            return pltpu.make_async_copy(
                tok_in.at[rows(m), cols(j)], x_ref.at[m, core * vchunks + j], tok_sem.at[m]
            )

        @pl.when(sec == 0)
        def _():
            for m in range(windows):
                for j in range(vchunks):
                    tok_load(m, j).start()

        small = [
            pltpu.make_async_copy(source, target, small_sem.at[i])
            for i, (source, target) in enumerate(
                (
                    (gain_in, gain_ref),
                    (start_in, start_ref),
                    (pad_in, pad_ref),
                    (cq_in, cq_ref),
                    (ck_in, ck_ref),
                    (cv_in, cv_ref),
                    (vg_in, vg_ref),
                )
            )
        ]
        for load in small:
            load.start()

        pltpu.make_async_copy(wq_ref.at[0], w_all.at[0, :, pl.ds(0, HD)], w_sem.at[0]).start()
        pltpu.make_async_copy(wk_ref.at[0], w_all.at[0, :, pl.ds(HD, HD)], w_sem.at[0]).start()
        for j in range(vchunks):
            pltpu.make_async_copy(wv_ref.at[0, :, cols(j)], w_all.at[1 + j], w_sem.at[1 + j]).start()

        def weights_ready(j):
            pltpu.make_async_copy(w_all.at[j], w_all.at[j], w_sem.at[j]).wait()

        barrier = pltpu.get_barrier_semaphore()
        pl.semaphore_signal(barrier, inc=1, device_id={"head": mate}, device_id_type=MESH)

        @pl.when(ctx > 0)
        def _():
            pl.semaphore_signal(barrier, inc=1, device_id={"ctx": ctx - 1}, device_id_type=MESH)

        @pl.when(ctx < ctx_n - 1)
        def _():
            pl.semaphore_signal(barrier, inc=1, device_id={"ctx": ctx + 1}, device_id_type=MESH)

        @pl.when(sec > 0)
        def _():
            pl.semaphore_signal(barrier, inc=1, device_id={"section": sec - 1}, device_id_type=MESH)

        @pl.when(sec < sec_n - 1)
        def _():
            pl.semaphore_signal(barrier, inc=1, device_id={"section": sec + 1}, device_id_type=MESH)

        first = ctx * span
        lead_pos = lax.broadcasted_iota(jnp.int32, (1, span), 1) + first
        col_pos = lax.broadcasted_iota(jnp.int32, (span, HD), 0) + first
        lane = lax.broadcasted_iota(jnp.int32, (1, HD), 1)
        low_half = lane < HD // 2
        lane_head = (lax.broadcasted_iota(jnp.int32, (1, 2 * HD), 1) % (HD // 2)) // FD

        @pl.when(ctx == 0)
        def _():
            for m in range(windows):
                pr_ref[m, :, pl.ds(0, 8), :] = jnp.zeros((heads + wide, 8, HD), F32)

            def clear(i, carry):
                got_ref[i // heads, i % heads] = jnp.zeros((FROWS, HD), BF16)
                return carry

            lax.fori_loop(0, windows * heads, clear, 0)

        peers = (
            1
            + jnp.where(ctx > 0, 1, 0)
            + jnp.where(ctx < ctx_n - 1, 1, 0)
            + jnp.where(sec > 0, 1, 0)
            + jnp.where(sec < sec_n - 1, 1, 0)
        )
        pl.semaphore_wait(barrier, peers)

        def remote(source, target, send, recv, where):
            return pltpu.make_async_remote_copy(
                src_ref=source, dst_ref=target, send_sem=send, recv_sem=recv, device_id=where, device_id_type=MESH
            )

        after_ctx = {"ctx": ctx + 1}

        def section_copy(m, j):
            return remote(
                out_ref.at[rows(m), cols(j)], x_ref.at[m, core * vchunks + j], sec_send, sec_recv.at[m, j], {"section": sec + 1}
            )

        def mate_copy(m, j):
            at = x_ref.at[m, core * vchunks + j]
            return remote(at, at, x_send, x_recv.at[m], {"head": mate})

        def mate_wait(m):
            at = x_ref.at[m, mate_at]
            remote(at, at, x_send, x_recv.at[m], {"head": mate}).wait_recv()

        def halo_copy(m, i):
            at = pl.ds(2 * i, 2 if i == 0 else vchunks - 1)
            return remote(ho_ref.at[m, at], hi_ref.at[m, at], halo_send, halo_recv.at[m, i], after_ctx)

        def piece(p):
            return pl.ds(pl.multiple_of(p * (FROWS // PIECES), FROWS // PIECES), FROWS // PIECES)

        def state_copy(m, h, p):
            return remote(
                fwd_ref.at[m, h, piece(p)], got_ref.at[m, h, piece(p)], st_send, st_recv.at[m, h, p], after_ctx
            )

        def part_copy(m, j):
            return remote(part_ref.at[m, j], other_ref.at[m, j], p_send, p_recv.at[m, j], {"head": mate})

        @pl.when(sec == 0)
        def _():
            for m in range(windows):
                at = x_ref.at[m, mine_at]
                pltpu.make_async_copy(at, at, tok_sem.at[m]).wait()
                for j in range(vchunks):
                    mate_copy(m, j).start()

        def exchange(m):
            @pl.when(sec > 0)
            def _():
                for j in range(vchunks):
                    section_copy(m, j).wait_recv()
                    mate_copy(m, j).start()

        for load in small:
            load.wait()

        def normalise(m):
            total = None
            for k in range(2 * vchunks):
                value = x_ref[m, k].astype(F32)
                square = value * value
                for c in range(wide):
                    part = square[:, c * HD : (c + 1) * HD]
                    total = part if total is None else total + part
            scale = lax.rsqrt(jnp.sum(total, axis=1, keepdims=True) * (1.0 / width) + EPS)
            for k in range(2 * vchunks):
                gain = gain_ref[:, cols(k)].astype(F32)
                n_ref[m, k] = (x_ref[m, k].astype(F32) * scale * gain).astype(BF16)

        def project(ms, j):
            rows_in = jnp.concatenate(
                [jnp.concatenate([n_ref[m, k] for k in range(2 * vchunks)], axis=1) for m in ms], axis=0
            )
            got = jnp.dot(rows_in, w_all[j], preferred_element_type=F32).astype(BF16).astype(F32)
            for i, m in enumerate(ms):
                for c in range(wide):
                    own = got[i * span : (i + 1) * span, c * HD : (c + 1) * HD]
                    pr_ref[m, wide * j + c, pl.ds(8, span), :] = own
                    ho_ref[m, j, pl.ds(4 * c, 4), :] = own[span - 4 :]

        def halo_send_off(m, i):
            @pl.when(ctx < ctx_n - 1)
            def _():
                halo_copy(m, i).start()

        def halo_wait(m, i):
            @pl.when(ctx > 0)
            def _():
                halo_copy(m, i).wait_recv()
                for j in range(2) if i == 0 else range(2, vchunks + 1):
                    for c in range(wide):
                        pr_ref[m, wide * j + c, pl.ds(4, 4), :] = hi_ref[m, j, pl.ds(4 * c, 4), :]

        def conv(m, c, taps_ref, tap_at, since):
            total = taps_ref[0, pl.ds(0, 1), tap_at].astype(F32) * pr_ref[m, c, pl.ds(8, span), :]
            for j in range(1, taps):
                term = taps_ref[0, pl.ds(j, 1), tap_at].astype(F32) * pr_ref[m, c, pl.ds(8 - j, span), :]
                total = total + jnp.where(since >= j, term, 0.0)
            return total

        def prepare(m):
            mate_wait(m)
            normalise(m)

            @pl.when(m == 0)
            def _():
                weights_ready(0)
                weights_ready(1)

            project([m], 0)
            project([m], 1)
            halo_send_off(m, 0)

            @pl.when(m == 0)
            def _():
                for j in range(2, vchunks + 1):
                    weights_ready(j)
                for j in range(2 * vchunks):
                    pltpu.make_async_copy(wo_ref.at[0, :, cols(j)], wo_v.at[j], w_sem.at[1 + vchunks]).start()

            for j in range(2, vchunks + 1):
                project([m], j)
            halo_send_off(m, 1)

        def inside(m):
            return jnp.logical_and(start_ref[m] >= first, start_ref[m] < first + span)

        def used_of(m):
            return jnp.where(jnp.logical_or(lead_pos < start_ref[m], start_ref[m] < first), 1.0, 0.0)

        def arrive(m):
            start = start_ref[m]
            since = col_pos - start
            since = jnp.where(since < 0, taps, since)
            kept = jnp.where(jnp.logical_or(lead_pos >= start, jnp.logical_not(inside(m))), 1.0, 0.0)
            used = used_of(m)

            def conv_query_key():
                for which, taps_ref, wide_ref, turned_ref, lead in (
                    (1, ck_ref, k3_ref, kt_ref, kept),
                    (0, cq_ref, q3_ref, qt_ref, used),
                ):
                    part = conv(m, which, taps_ref, pl.ds(0, HD), since)
                    turned = jnp.transpose(part) * (0.5 * lead)
                    for h in range(heads):
                        own = turned[h * FD : (h + 1) * FD]
                        turned_ref[h, pl.ds(0, FD), :] = own
                        turned_ref[h, pl.ds(FD, FD), :] = own
                    if which == 0:
                        part = part * (1.0 / math.sqrt(FD))
                    rolled = pltpu.roll(part, HD // 2, 1)
                    for g in range(2):
                        both = jnp.where(low_half, part, rolled) if g == 0 else jnp.where(low_half, rolled, part)
                        high = both.astype(BF16).astype(F32)
                        low = both - high
                        if which == 0:
                            wide_ref[g, :, pl.ds(0, HD)] = high.astype(BF16)
                            wide_ref[g, :, pl.ds(HD, HD)] = low.astype(BF16)
                        else:
                            wide_ref[g, :, pl.ds(0, HD)] = jnp.where(low_half, high, low).astype(BF16)
                            wide_ref[g, :, pl.ds(HD, HD)] = jnp.where(low_half, high, 0.0).astype(BF16)

            def values(h):
                at = pl.ds((h % wide) * HD, HD)
                v_ref[h // wide, :, at] = conv(m, wide + h, cv_ref, pl.ds(h * HD, HD), since).astype(BF16)
                made = jnp.dot(features(kt_ref, h, kept), v_ref[h // wide, :, at], preferred_element_type=F32)
                fwd_ref[m, h] = made.astype(BF16)
                bs_ref[m, h] = made

            def send_states(low, high):
                if ctx_n > 1:

                    @pl.when(ctx == 0)
                    def _():
                        for h in range(low, high):
                            for p in range(PIECES):
                                state_copy(m, h, p).start()

            halo_wait(m, 0)
            halo_wait(m, 1)
            conv_query_key()
            for h in range(heads // 2):
                values(h)
            send_states(0, heads // 2)
            for h in range(heads // 2, heads):
                values(h)
            send_states(heads // 2, heads)

        def within(m):
            start = start_ref[m]
            used = used_of(m)
            edge = start - first
            row_pos = lax.broadcasted_iota(jnp.int32, (span, span), 0)
            other_pos = lax.broadcasted_iota(jnp.int32, (span, span), 1)
            allowed = jnp.logical_and(other_pos <= row_pos, (other_pos >= edge) == (row_pos >= edge))
            mask_ref[...] = jnp.where(allowed, 1.0, 0.0).astype(BF16)

            for g in range(2):
                stacked = jnp.concatenate(
                    [jnp.where(lane_head == c, q3_ref[g], jnp.zeros((), BF16)) for c in range(heads // 2)], axis=0
                )
                s_all = lax.dot_general(stacked, k3_ref[g], (((1,), (1,)), ((), ())), preferred_element_type=F32)
                for c in range(heads // 2):
                    h = g * (heads // 2) + c
                    s = s_all[c * span : (c + 1) * span]
                    weight = ((0.5 * s + 1.0) * s + 1.0).astype(BF16) * mask_ref[...]
                    num_ref[m, h] = jnp.dot(
                        weight, v_ref[h // wide, :, pl.ds((h % wide) * HD, HD)], preferred_element_type=F32
                    )
                    qf_ref[m, h] = jnp.transpose(features(qt_ref, h, used))

        def states_pass(m):
            reset = inside(m)

            def chain(i, carry):
                h, p = i // PIECES, i % PIECES

                @pl.when(ctx > 0)
                def _():
                    state_copy(m, h, p).wait_recv()

                @pl.when(jnp.logical_and(ctx > 0, ctx < ctx_n - 1))
                def _():
                    old = got_ref[m, h, piece(p), :].astype(F32)
                    fwd_ref[m, h, piece(p), :] = (bs_ref[m, h, piece(p), :] + jnp.where(reset, 0.0, old)).astype(BF16)
                    state_copy(m, h, p).start()

                return carry

            lax.fori_loop(0, heads * PIECES, chain, 0)

        def mix(m):
            for h in range(heads):
                num = num_ref[m, h] + jnp.dot(qf_ref[m, h], got_ref[m, h], preferred_element_type=F32)
                square = jnp.mean(num * num, axis=1, keepdims=True)
                mix_ref[h // wide, :, pl.ds((h % wide) * HD, HD)] = (
                    num * lax.rsqrt(square + EPS) * vg_ref[:, pl.ds(h * HD, HD)].astype(F32)
                ).astype(BF16)

        def output(m):
            @pl.when(m == 0)
            def _():
                pltpu.make_async_copy(wo_v, wo_v, w_sem.at[1 + vchunks]).wait()

            def mixed():
                return jnp.concatenate([mix_ref[k] for k in range(vchunks)], axis=1)

            for j in range(vchunks):
                part_ref[m, j] = jnp.dot(mixed(), wo_v[mate * vchunks + j], preferred_element_type=F32).astype(BF16)
            for j in range(vchunks):
                part_copy(m, j).start()
            for j in range(vchunks):
                own_ref[j] = jnp.dot(mixed(), wo_v[core * vchunks + j], preferred_element_type=F32)
            valid = first + lax.broadcasted_iota(jnp.int32, (span, CHUNK), 0) < span * ctx_n - pad_ref[m]
            for j in range(vchunks):
                part_copy(m, j).wait_recv()
                update = jnp.where(valid, own_ref[j] + other_ref[m, j].astype(F32), 0.0)
                out_ref[rows(m), cols(j)] = (x_ref[m, core * vchunks + j].astype(F32) + update).astype(BF16)

                @pl.when(sec < sec_n - 1)
                def _():
                    section_copy(m, j).start()


        last = ctx == ctx_n - 1
        out_turn = jnp.where(sec == 0, 0, jnp.where(last, 1, 2))
        local_turn = jnp.where(last, 0, 0)

        def step(t, carry):
            here = t < windows

            def turn(u, carry):
                @pl.when(jnp.logical_and(u == out_turn, t > 0))
                def _():
                    output(t - 1)

                @pl.when(jnp.logical_and(u == 0, here))
                def _():
                    exchange(t)

                    def slot(v, carry):
                        now = jnp.logical_and(v == 0, jnp.logical_or(sec > 0, t == 0))
                        ahead = jnp.logical_and(v == 1, sec == 0)

                        @pl.when(jnp.logical_and(jnp.logical_or(now, ahead), t + v < windows))
                        def _():
                            prepare(t + v)

                        @pl.when(v == 0)
                        def _():
                            arrive(t)

                        return carry

                    lax.fori_loop(0, 2, slot, 0)

                @pl.when(jnp.logical_and(u == local_turn, here))
                def _():
                    within(t)

                @pl.when(jnp.logical_and(u == 1, here))
                def _():
                    states_pass(t)

                @pl.when(jnp.logical_and(u == 2, here))
                def _():
                    mix(t)

                return carry

            lax.fori_loop(0, 3, turn, 0)
            return carry

        lax.fori_loop(0, windows + 1, step, 0)

        def sent(ref, sem):
            remote(ref, ref, sem, sem, {"head": mate}).wait_send()

        sent(x_ref.at[:, mine_at], x_send)
        sent(part_ref, p_send)

        @pl.when(sec < sec_n - 1)
        def _():
            sent(out_ref, sec_send)

        @pl.when(ctx < ctx_n - 1)
        def _():
            sent(ho_ref, halo_send)
            sent(fwd_ref, st_send)

    return kernel


def local(
    tokens, norm_gain, w_query, w_key, w_value, conv_query, conv_key, conv_value, value_gain, w_out, doc_start, pad_length
):
    windows, span, half = tokens.shape
    width = 2 * half
    rows_n = windows * span
    heads = half // HD
    vchunks = half // CHUNK
    sizes = (lax.axis_size("ctx"), lax.axis_size("section"), windows, span, width, conv_query.shape[1])
    hbm = pl.BlockSpec(memory_space=pltpu.MemorySpace.HBM)
    dma = pltpu.SemaphoreType.DMA
    vmem = pltpu.VMEM
    out = pl.pallas_call(
        make_kernel(sizes),
        out_shape=pltpu.VMEM((rows_n, half), BF16),
        in_specs=[hbm] * 12,
        out_specs=pl.BlockSpec(memory_space=pltpu.VMEM),
        scratch_shapes=[
            pltpu.SMEM((windows,), jnp.int32),
            pltpu.SMEM((windows,), jnp.int32),
            vmem(norm_gain.shape, BF16),
            vmem(conv_query.shape, BF16),
            vmem(conv_key.shape, BF16),
            vmem(conv_value.shape, BF16),
            vmem(value_gain.shape, BF16),
            dma((7,)),
            vmem((vchunks + 1, width, CHUNK), BF16),
            vmem((2 * vchunks, half, CHUNK), BF16),
            vmem((windows, 2 * vchunks, span, CHUNK), BF16),
            vmem((windows, 2 * vchunks, span, CHUNK), BF16),
            vmem((windows, heads + CHUNK // HD, span + 8, HD), F32),
            vmem((windows, vchunks + 1, 8, HD), F32),
            vmem((windows, vchunks + 1, 8, HD), F32),
            vmem((2, span, 2 * HD), BF16),
            vmem((2, span, 2 * HD), BF16),
            vmem((heads, 2 * FD, span), F32),
            vmem((heads, 2 * FD, span), F32),
            vmem((vchunks, span, CHUNK), BF16),
            vmem((windows, heads, FROWS, HD), F32),
            vmem((windows, heads, FROWS, HD), BF16),
            vmem((windows, heads, FROWS, HD), BF16),
            vmem((windows, heads, span, FROWS), BF16),
            vmem((windows, heads, span, HD), F32),
            vmem((vchunks, span, CHUNK), BF16),
            vmem((span, span), BF16),
            vmem((windows, vchunks, span, CHUNK), BF16),
            vmem((windows, vchunks, span, CHUNK), BF16),
            vmem((vchunks, span, CHUNK), F32),
            dma((2 + vchunks,)),
            dma((windows,)),
            dma(()),
            dma((windows,)),
            dma(()),
            dma((windows, vchunks)),
            dma(()),
            dma((windows, 2)),
            dma(()),
            dma((windows, heads, PIECES)),
            dma(()),
            dma((windows, vchunks)),
        ],
        compiler_params=pltpu.CompilerParams(
            collective_id=0, has_side_effects=True, vmem_limit_bytes=60 * 1024 * 1024
        ),
        name="layers",
    )(
        doc_start, pad_length, tokens.reshape(rows_n, half), norm_gain, w_query, w_key, w_value,
        conv_query, conv_key, conv_value, value_gain, w_out,
    )
    return out.reshape(1, windows, span, half)


def solution(mesh):
    return jax.shard_map(
        local,
        mesh=mesh,
        in_specs=(
            P("groups", "ctx", "head"),
            P("section", None),
            P("section", None, "head"),
            P("section", None, "head"),
            P("section", None, "head"),
            P("section", None, "head"),
            P("section", None, "head"),
            P("section", None, "head"),
            P("section", "head"),
            P("section", "head", None),
            P("groups"),
            P("groups"),
        ),
        out_specs=P("section", "groups", "ctx", "head"),
        check_vma=False,
    )
```

```python
import math

import jax
import jax.numpy as jnp
from jax import lax
from jax.experimental import pallas as pl
from jax.experimental.pallas import tpu as pltpu
from jax.sharding import PartitionSpec as P

HD = 128
FD = 16
FROWS = 160
PIECES = 2
CHUNK = 256
EPS = 1e-06
MESH = pl.DeviceIdType.MESH
F32 = jnp.float32
BF16 = jnp.bfloat16


def features(doubled, h, lead):
    y = doubled[h, pl.ds(0, FD), :]
    rows = [y, y * y * math.sqrt(0.5)]
    for d in range(1, FD // 2):
        rows.append(y * doubled[h, pl.ds(d, FD), :])
    half = FD // 2
    rows.append(y[:half] * y[half:])
    top = lax.broadcasted_iota(jnp.int32, (half, y.shape[1]), 0) == 0
    rows.append(jnp.where(top, lead, 0.0))
    return jnp.concatenate(rows, axis=0).astype(BF16)


def make_kernel(sizes):
    ctx_n, sec_n, windows, span, width, taps = sizes
    half = width // 2
    heads = half // HD
    vchunks = half // CHUNK
    pair = heads // vchunks
    wide = CHUNK // HD

    def kernel(
        start_in, pad_in, tok_in, gain_in, wq_ref, wk_ref, wv_ref, cq_in, ck_in, cv_in, vg_in, wo_ref,
        out_ref,
        start_ref, pad_ref, gain_ref, cq_ref, ck_ref, cv_ref, vg_ref, small_sem,
        w_all, wo_v, x_ref, n_ref, pr_ref, ho_ref, hi_ref, q3_ref, k3_ref, qt_ref, kt_ref, v_ref,
        bs_ref, got_ref, fwd_ref, qf_ref, num_ref, mix_ref, mask_ref, part_ref, other_ref, own_ref,
        w_sem, tok_sem, x_send, x_recv, sec_send, sec_recv, halo_send, halo_recv, st_send, st_recv,
        p_send, p_recv,
    ):
        ctx = lax.axis_index("ctx")
        sec = lax.axis_index("section")
        core = lax.axis_index("head")
        mate = 1 - core
        mine_at = pl.ds(core * vchunks, vchunks)
        mate_at = pl.ds(mate * vchunks, vchunks)

        def cols(j):
            return pl.ds(j * CHUNK, CHUNK)

        def rows(m):
            return pl.ds(pl.multiple_of(m * span, span), span)

        def tok_load(m, j):
            return pltpu.make_async_copy(
                tok_in.at[rows(m), cols(j)], x_ref.at[m, core * vchunks + j], tok_sem.at[m]
            )

        @pl.when(sec == 0)
        def _():
            for m in range(windows):
                for j in range(vchunks):
                    tok_load(m, j).start()

        small = [
            pltpu.make_async_copy(source, target, small_sem.at[i])
            for i, (source, target) in enumerate(
                (
                    (gain_in, gain_ref),
                    (start_in, start_ref),
                    (pad_in, pad_ref),
                    (cq_in, cq_ref),
                    (ck_in, ck_ref),
                    (cv_in, cv_ref),
                    (vg_in, vg_ref),
                )
            )
        ]
        for load in small:
            load.start()

        pltpu.make_async_copy(wq_ref.at[0], w_all.at[0, :, pl.ds(0, HD)], w_sem.at[0]).start()
        pltpu.make_async_copy(wk_ref.at[0], w_all.at[0, :, pl.ds(HD, HD)], w_sem.at[0]).start()
        for j in range(vchunks):
            pltpu.make_async_copy(wv_ref.at[0, :, cols(j)], w_all.at[1 + j], w_sem.at[1 + j]).start()

        def weights_ready(j):
            pltpu.make_async_copy(w_all.at[j], w_all.at[j], w_sem.at[j]).wait()

        barrier = pltpu.get_barrier_semaphore()
        pl.semaphore_signal(barrier, inc=1, device_id={"head": mate}, device_id_type=MESH)

        @pl.when(ctx > 0)
        def _():
            pl.semaphore_signal(barrier, inc=1, device_id={"ctx": ctx - 1}, device_id_type=MESH)

        @pl.when(ctx < ctx_n - 1)
        def _():
            pl.semaphore_signal(barrier, inc=1, device_id={"ctx": ctx + 1}, device_id_type=MESH)

        @pl.when(sec > 0)
        def _():
            pl.semaphore_signal(barrier, inc=1, device_id={"section": sec - 1}, device_id_type=MESH)

        @pl.when(sec < sec_n - 1)
        def _():
            pl.semaphore_signal(barrier, inc=1, device_id={"section": sec + 1}, device_id_type=MESH)

        first = ctx * span
        lead_pos = lax.broadcasted_iota(jnp.int32, (1, span), 1) + first
        col_pos = lax.broadcasted_iota(jnp.int32, (span, HD), 0) + first
        lane = lax.broadcasted_iota(jnp.int32, (1, HD), 1)
        low_half = lane < HD // 2
        lane_head = (lax.broadcasted_iota(jnp.int32, (1, 2 * HD), 1) % (HD // 2)) // FD

        @pl.when(ctx == 0)
        def _():
            for m in range(windows):
                pr_ref[m, :, pl.ds(0, 8), :] = jnp.zeros((heads + wide, 8, HD), F32)

            def clear(i, carry):
                got_ref[i // heads, i % heads] = jnp.zeros((FROWS, HD), BF16)
                return carry

            lax.fori_loop(0, windows * heads, clear, 0)

        peers = (
            1
            + jnp.where(ctx > 0, 1, 0)
            + jnp.where(ctx < ctx_n - 1, 1, 0)
            + jnp.where(sec > 0, 1, 0)
            + jnp.where(sec < sec_n - 1, 1, 0)
        )
        pl.semaphore_wait(barrier, peers)

        def remote(source, target, send, recv, where):
            return pltpu.make_async_remote_copy(
                src_ref=source, dst_ref=target, send_sem=send, recv_sem=recv, device_id=where, device_id_type=MESH
            )

        after_ctx = {"ctx": ctx + 1}

        def section_copy(m, j):
            return remote(
                out_ref.at[rows(m), cols(j)], x_ref.at[m, core * vchunks + j], sec_send, sec_recv.at[m, j], {"section": sec + 1}
            )

        def mate_copy(m, j):
            at = x_ref.at[m, core * vchunks + j]
            return remote(at, at, x_send, x_recv.at[m], {"head": mate})

        def mate_wait(m):
            at = x_ref.at[m, mate_at]
            remote(at, at, x_send, x_recv.at[m], {"head": mate}).wait_recv()

        def halo_copy(m, i):
            at = pl.ds(2 * i, 2 if i == 0 else vchunks - 1)
            return remote(ho_ref.at[m, at], hi_ref.at[m, at], halo_send, halo_recv.at[m, i], after_ctx)

        def piece(p):
            return pl.ds(pl.multiple_of(p * (FROWS // PIECES), FROWS // PIECES), FROWS // PIECES)

        def state_copy(m, h, p):
            return remote(
                fwd_ref.at[m, h, piece(p)], got_ref.at[m, h, piece(p)], st_send, st_recv.at[m, h, p], after_ctx
            )

        def part_copy(m, j):
            return remote(part_ref.at[m, j], other_ref.at[m, j], p_send, p_recv.at[m, j], {"head": mate})

        @pl.when(sec == 0)
        def _():
            for m in range(windows):
                at = x_ref.at[m, mine_at]
                pltpu.make_async_copy(at, at, tok_sem.at[m]).wait()
                for j in range(vchunks):
                    mate_copy(m, j).start()

        def exchange(m):
            @pl.when(sec > 0)
            def _():
                for j in range(vchunks):
                    section_copy(m, j).wait_recv()
                    mate_copy(m, j).start()

        for load in small:
            load.wait()

        def normalise(m):
            total = None
            for k in range(2 * vchunks):
                value = x_ref[m, k].astype(F32)
                square = value * value
                for c in range(wide):
                    part = square[:, c * HD : (c + 1) * HD]
                    total = part if total is None else total + part
            scale = lax.rsqrt(jnp.sum(total, axis=1, keepdims=True) * (1.0 / width) + EPS)
            for k in range(2 * vchunks):
                gain = gain_ref[:, cols(k)].astype(F32)
                n_ref[m, k] = (x_ref[m, k].astype(F32) * scale * gain).astype(BF16)

        def project(ms, j):
            rows_in = jnp.concatenate(
                [jnp.concatenate([n_ref[m, k] for k in range(2 * vchunks)], axis=1) for m in ms], axis=0
            )
            got = jnp.dot(rows_in, w_all[j], preferred_element_type=F32).astype(BF16).astype(F32)
            for i, m in enumerate(ms):
                for c in range(wide):
                    own = got[i * span : (i + 1) * span, c * HD : (c + 1) * HD]
                    pr_ref[m, wide * j + c, pl.ds(8, span), :] = own
                    ho_ref[m, j, pl.ds(4 * c, 4), :] = own[span - 4 :]

        def halo_send_off(m, i):
            @pl.when(ctx < ctx_n - 1)
            def _():
                halo_copy(m, i).start()

        def halo_wait(m, i):
            @pl.when(ctx > 0)
            def _():
                halo_copy(m, i).wait_recv()
                for j in range(2) if i == 0 else range(2, vchunks + 1):
                    for c in range(wide):
                        pr_ref[m, wide * j + c, pl.ds(4, 4), :] = hi_ref[m, j, pl.ds(4 * c, 4), :]

        def conv(m, c, taps_ref, tap_at, since):
            total = taps_ref[0, pl.ds(0, 1), tap_at].astype(F32) * pr_ref[m, c, pl.ds(8, span), :]
            for j in range(1, taps):
                term = taps_ref[0, pl.ds(j, 1), tap_at].astype(F32) * pr_ref[m, c, pl.ds(8 - j, span), :]
                total = total + jnp.where(since >= j, term, 0.0)
            return total

        def prepare(m):
            mate_wait(m)
            normalise(m)

            @pl.when(m == 0)
            def _():
                weights_ready(0)
                weights_ready(1)

            project([m], 0)
            project([m], 1)
            halo_send_off(m, 0)

            @pl.when(m == 0)
            def _():
                for j in range(2, vchunks + 1):
                    weights_ready(j)
                for j in range(2 * vchunks):
                    pltpu.make_async_copy(wo_ref.at[0, :, cols(j)], wo_v.at[j], w_sem.at[1 + vchunks]).start()

            for j in range(2, vchunks + 1):
                project([m], j)
            halo_send_off(m, 1)

        def inside(m):
            return jnp.logical_and(start_ref[m] >= first, start_ref[m] < first + span)

        def used_of(m):
            return jnp.where(jnp.logical_or(lead_pos < start_ref[m], start_ref[m] < first), 1.0, 0.0)

        def arrive(m):
            start = start_ref[m]
            since = col_pos - start
            since = jnp.where(since < 0, taps, since)
            kept = jnp.where(jnp.logical_or(lead_pos >= start, jnp.logical_not(inside(m))), 1.0, 0.0)
            used = used_of(m)

            def conv_query_key():
                for which, taps_ref, wide_ref, turned_ref, lead in (
                    (1, ck_ref, k3_ref, kt_ref, kept),
                    (0, cq_ref, q3_ref, qt_ref, used),
                ):
                    part = conv(m, which, taps_ref, pl.ds(0, HD), since)
                    turned = jnp.transpose(part) * (0.5 * lead)
                    for h in range(heads):
                        own = turned[h * FD : (h + 1) * FD]
                        turned_ref[h, pl.ds(0, FD), :] = own
                        turned_ref[h, pl.ds(FD, FD), :] = own
                    if which == 0:
                        part = part * (1.0 / math.sqrt(FD))
                    rolled = pltpu.roll(part, HD // 2, 1)
                    for g in range(2):
                        both = jnp.where(low_half, part, rolled) if g == 0 else jnp.where(low_half, rolled, part)
                        high = both.astype(BF16).astype(F32)
                        low = both - high
                        if which == 0:
                            wide_ref[g, :, pl.ds(0, HD)] = high.astype(BF16)
                            wide_ref[g, :, pl.ds(HD, HD)] = low.astype(BF16)
                        else:
                            wide_ref[g, :, pl.ds(0, HD)] = jnp.where(low_half, high, low).astype(BF16)
                            wide_ref[g, :, pl.ds(HD, HD)] = jnp.where(low_half, high, 0.0).astype(BF16)

            def values(h):
                at = pl.ds((h % wide) * HD, HD)
                v_ref[h // wide, :, at] = conv(m, wide + h, cv_ref, pl.ds(h * HD, HD), since).astype(BF16)
                made = jnp.dot(features(kt_ref, h, kept), v_ref[h // wide, :, at], preferred_element_type=F32)
                fwd_ref[m, h] = made.astype(BF16)
                bs_ref[m, h] = made

            def send_states(low, high):
                if ctx_n > 1:

                    @pl.when(ctx == 0)
                    def _():
                        for h in range(low, high):
                            for p in range(PIECES):
                                state_copy(m, h, p).start()

            halo_wait(m, 0)
            halo_wait(m, 1)
            conv_query_key()
            for h in range(heads // 2):
                values(h)
            send_states(0, heads // 2)
            for h in range(heads // 2, heads):
                values(h)
            send_states(heads // 2, heads)

        def within(m):
            start = start_ref[m]
            used = used_of(m)
            edge = start - first
            row_pos = lax.broadcasted_iota(jnp.int32, (span, span), 0)
            other_pos = lax.broadcasted_iota(jnp.int32, (span, span), 1)
            allowed = jnp.logical_and(other_pos <= row_pos, (other_pos >= edge) == (row_pos >= edge))
            mask_ref[...] = jnp.where(allowed, 1.0, 0.0).astype(BF16)

            for g in range(2):
                stacked = jnp.concatenate(
                    [jnp.where(lane_head == c, q3_ref[g], jnp.zeros((), BF16)) for c in range(heads // 2)], axis=0
                )
                s_all = lax.dot_general(stacked, k3_ref[g], (((1,), (1,)), ((), ())), preferred_element_type=F32)
                for c in range(heads // 2):
                    h = g * (heads // 2) + c
                    s = s_all[c * span : (c + 1) * span]
                    weight = ((0.5 * s + 1.0) * s + 1.0).astype(BF16) * mask_ref[...]
                    num_ref[m, h] = jnp.dot(
                        weight, v_ref[h // wide, :, pl.ds((h % wide) * HD, HD)], preferred_element_type=F32
                    )
                    qf_ref[m, h] = jnp.transpose(features(qt_ref, h, used))

        def states_pass(m):
            reset = inside(m)

            def chain(i, carry):
                h, p = i // PIECES, i % PIECES

                @pl.when(jnp.logical_and(i == 6, jnp.logical_and(sec == 0, m < windows - 1)))
                def _():
                    prepare(m + 1)

                @pl.when(ctx > 0)
                def _():
                    state_copy(m, h, p).wait_recv()

                @pl.when(jnp.logical_and(ctx > 0, ctx < ctx_n - 1))
                def _():
                    old = got_ref[m, h, piece(p), :].astype(F32)
                    fwd_ref[m, h, piece(p), :] = (bs_ref[m, h, piece(p), :] + jnp.where(reset, 0.0, old)).astype(BF16)
                    state_copy(m, h, p).start()

                return carry

            lax.fori_loop(0, heads * PIECES, chain, 0)

        def mix(m):
            for h in range(heads):
                num = num_ref[m, h] + jnp.dot(qf_ref[m, h], got_ref[m, h], preferred_element_type=F32)
                square = jnp.mean(num * num, axis=1, keepdims=True)
                mix_ref[h // wide, :, pl.ds((h % wide) * HD, HD)] = (
                    num * lax.rsqrt(square + EPS) * vg_ref[:, pl.ds(h * HD, HD)].astype(F32)
                ).astype(BF16)

        def output(m):
            @pl.when(m == 0)
            def _():
                pltpu.make_async_copy(wo_v, wo_v, w_sem.at[1 + vchunks]).wait()

            def mixed():
                return jnp.concatenate([mix_ref[k] for k in range(vchunks)], axis=1)

            for j in range(vchunks):
                part_ref[m, j] = jnp.dot(mixed(), wo_v[mate * vchunks + j], preferred_element_type=F32).astype(BF16)
            for j in range(vchunks):
                part_copy(m, j).start()
            for j in range(vchunks):
                own_ref[j] = jnp.dot(mixed(), wo_v[core * vchunks + j], preferred_element_type=F32)
            valid = first + lax.broadcasted_iota(jnp.int32, (span, CHUNK), 0) < span * ctx_n - pad_ref[m]
            for j in range(vchunks):
                part_copy(m, j).wait_recv()
                update = jnp.where(valid, own_ref[j] + other_ref[m, j].astype(F32), 0.0)
                out_ref[rows(m), cols(j)] = (x_ref[m, core * vchunks + j].astype(F32) + update).astype(BF16)

                @pl.when(sec < sec_n - 1)
                def _():
                    section_copy(m, j).start()


        last = ctx == ctx_n - 1
        out_turn = jnp.where(sec == 0, 0, jnp.where(last, 1, 2))
        local_turn = jnp.where(last, 0, 0)

        def step(t, carry):
            here = t < windows

            def turn(u, carry):
                @pl.when(jnp.logical_and(u == out_turn, t > 0))
                def _():
                    output(t - 1)

                @pl.when(jnp.logical_and(u == 0, here))
                def _():
                    exchange(t)

                    def slot(v, carry):
                        now = jnp.logical_and(v == 0, jnp.logical_or(sec > 0, t == 0))

                        @pl.when(now)
                        def _():
                            prepare(t)

                        @pl.when(v == 0)
                        def _():
                            arrive(t)

                        return carry

                    lax.fori_loop(0, 2, slot, 0)

                @pl.when(jnp.logical_and(u == local_turn, here))
                def _():
                    within(t)

                @pl.when(jnp.logical_and(u == 1, here))
                def _():
                    states_pass(t)

                @pl.when(jnp.logical_and(u == 2, here))
                def _():
                    mix(t)

                return carry

            lax.fori_loop(0, 3, turn, 0)
            return carry

        lax.fori_loop(0, windows + 1, step, 0)

        def sent(ref, sem):
            remote(ref, ref, sem, sem, {"head": mate}).wait_send()

        sent(x_ref.at[:, mine_at], x_send)
        sent(part_ref, p_send)

        @pl.when(sec < sec_n - 1)
        def _():
            sent(out_ref, sec_send)

        @pl.when(ctx < ctx_n - 1)
        def _():
            sent(ho_ref, halo_send)
            sent(fwd_ref, st_send)

    return kernel


def local(
    tokens, norm_gain, w_query, w_key, w_value, conv_query, conv_key, conv_value, value_gain, w_out, doc_start, pad_length
):
    windows, span, half = tokens.shape
    width = 2 * half
    rows_n = windows * span
    heads = half // HD
    vchunks = half // CHUNK
    sizes = (lax.axis_size("ctx"), lax.axis_size("section"), windows, span, width, conv_query.shape[1])
    hbm = pl.BlockSpec(memory_space=pltpu.MemorySpace.HBM)
    dma = pltpu.SemaphoreType.DMA
    vmem = pltpu.VMEM
    out = pl.pallas_call(
        make_kernel(sizes),
        out_shape=pltpu.VMEM((rows_n, half), BF16),
        in_specs=[hbm] * 12,
        out_specs=pl.BlockSpec(memory_space=pltpu.VMEM),
        scratch_shapes=[
            pltpu.SMEM((windows,), jnp.int32),
            pltpu.SMEM((windows,), jnp.int32),
            vmem(norm_gain.shape, BF16),
            vmem(conv_query.shape, BF16),
            vmem(conv_key.shape, BF16),
            vmem(conv_value.shape, BF16),
            vmem(value_gain.shape, BF16),
            dma((7,)),
            vmem((vchunks + 1, width, CHUNK), BF16),
            vmem((2 * vchunks, half, CHUNK), BF16),
            vmem((windows, 2 * vchunks, span, CHUNK), BF16),
            vmem((windows, 2 * vchunks, span, CHUNK), BF16),
            vmem((windows, heads + CHUNK // HD, span + 8, HD), F32),
            vmem((windows, vchunks + 1, 8, HD), F32),
            vmem((windows, vchunks + 1, 8, HD), F32),
            vmem((2, span, 2 * HD), BF16),
            vmem((2, span, 2 * HD), BF16),
            vmem((heads, 2 * FD, span), F32),
            vmem((heads, 2 * FD, span), F32),
            vmem((vchunks, span, CHUNK), BF16),
            vmem((windows, heads, FROWS, HD), F32),
            vmem((windows, heads, FROWS, HD), BF16),
            vmem((windows, heads, FROWS, HD), BF16),
            vmem((windows, heads, span, FROWS), BF16),
            vmem((windows, heads, span, HD), F32),
            vmem((vchunks, span, CHUNK), BF16),
            vmem((span, span), BF16),
            vmem((windows, vchunks, span, CHUNK), BF16),
            vmem((windows, vchunks, span, CHUNK), BF16),
            vmem((vchunks, span, CHUNK), F32),
            dma((2 + vchunks,)),
            dma((windows,)),
            dma(()),
            dma((windows,)),
            dma(()),
            dma((windows, vchunks)),
            dma(()),
            dma((windows, 2)),
            dma(()),
            dma((windows, heads, PIECES)),
            dma(()),
            dma((windows, vchunks)),
        ],
        compiler_params=pltpu.CompilerParams(
            collective_id=0, has_side_effects=True, vmem_limit_bytes=60 * 1024 * 1024
        ),
        name="layers",
    )(
        doc_start, pad_length, tokens.reshape(rows_n, half), norm_gain, w_query, w_key, w_value,
        conv_query, conv_key, conv_value, value_gain, w_out,
    )
    return out.reshape(1, windows, span, half)


def solution(mesh):
    return jax.shard_map(
        local,
        mesh=mesh,
        in_specs=(
            P("groups", "ctx", "head"),
            P("section", None),
            P("section", None, "head"),
            P("section", None, "head"),
            P("section", None, "head"),
            P("section", None, "head"),
            P("section", None, "head"),
            P("section", None, "head"),
            P("section", "head"),
            P("section", "head", None),
            P("groups"),
            P("groups"),
        ),
        out_specs=P("section", "groups", "ctx", "head"),
        check_vma=False,
    )
```
